32 devices in a mesh: gx: 4 (over y, core), gy: 8 (over z, x).
Axes of the slice: x: 2, y: 2, z: 4, core: 2. Of those that a mesh axis runs over, the one named last changes fastest.
Arguments:
- velocity: float32 [3, 32, 64, 128], P(None, 'gx', 'gy'), may hold values from -6 to 6
- viscosity: float32 [32, 64, 128], P('gx', 'gy'), may hold values from 0.02 to 0.16
- forcing: float32 [4, 3, 32, 64, 128], P(None, None, 'gx', 'gy'), may hold values from -6 to 6
- earlier: float32 [60, 3, 32, 64, 128], P(None, None, 'gx', 'gy'), may hold values from -12 to 12
Outputs:
- velocity_out: float32 [3, 32, 64, 128], P(None, 'gx', 'gy')
- basis: float32 [64, 3, 32, 64, 128], P(None, None, 'gx', 'gy')
- factor: float32 [64, 64], replicated
The draws below stay inside these ranges and needn't reach their ends.
All inputs are finite; a program needn't handle non-finite values.
Results may differ from the reference program's by a relative error of at most 0.000068.
Values sent between devices are 32-bit elements; how exact they have to be, the bound alone decides.
No kernel may reach another device: no remote copies, remote signals or barrier semaphores. Data moves between devices by JAX's collectives and lax.ppermute only.
A program may use at most 64 MiB of HBM per device.

```python
import math
import jax
import jax.numpy as jnp
from jax import lax

NZ = 128
K = 64
STEPS = 4
KEPT = 60
NX = 32
NY = 64


def draw_earlier(key, part):
    shape = (KEPT, 3, NX, NY, NZ)
    along_x = jnp.arange(NX, dtype=jnp.float32) / NX
    along_y = jnp.arange(NY, dtype=jnp.float32) / NY
    profile = 0.5 + 0.75 * (along_x[:, None] + along_y[None, :])
    profile = profile[None, None, :, :, None]
    values = jnp.clip(jax.random.normal(key, shape, jnp.float32), -6.0, 6.0) * profile
    return values.astype(jnp.float32)


def steps_of(stream_key, extent, shards, least, top_value):
    level, own = 1.0, jax.random.fold_in(stream_key, 6)
    for dim, shards_of in shards:
        steps = jnp.exp(jax.random.uniform(jax.random.fold_in(own, dim), (shards_of,), jnp.float32, least / len(shards), top_value / len(shards)))
        level = level * jnp.repeat(steps, extent[dim] // shards_of).reshape([-1 if axis == dim else 1 for axis in range(len(extent))])
    return level


def bell_draw(own_key, shape, scale, bound, pieces=(), held_as=jnp.bfloat16):
    loudness = steps_of(own_key, shape, pieces, -0.22, 0.18) if pieces else 1.0
    values = jax.random.normal(own_key, shape, jnp.float32) * scale * loudness
    return jnp.minimum(jnp.maximum(values, -bound), bound).astype(held_as)


def setup_inputs(seed: int = 0) -> dict:
    splits = jax.random.split(jax.random.key(seed), 5)
    velocity = bell_draw(splits[0], (3, NX, NY, NZ), 1.0, 6.0, ((1, 4), (2, 8)), jnp.float32)
    viscosity = jnp.clip(jnp.exp(math.log(0.16) - 2.0794415 * jax.random.uniform(splits[1], (NX, NY, NZ), jnp.float32) ** steps_of(splits[1], (NX, NY, NZ), ((0, 4), (1, 8)), -0.2, 0.2)), 0.02, 0.16)
    forcing = bell_draw(splits[2], (STEPS, 3, NX, NY, NZ), 1.0, 6.0, ((2, 4), (3, 8)), jnp.float32)
    earlier = draw_earlier(jax.random.fold_in(splits[4], 71), 0)
    return dict(velocity=velocity, viscosity=viscosity, forcing=forcing, earlier=earlier)


def laplace(padded, visc_pad):
    size_x = padded.shape[1] - 2
    size_y = padded.shape[2] - 2
    size_z = padded.shape[3] - 2
    centre = padded[:, 1:1 + size_x, 1:1 + size_y, 1:1 + size_z]
    visc_mid = visc_pad[1:1 + size_x, 1:1 + size_y, 1:1 + size_z]
    result = jnp.zeros_like(centre)
    for offset in ((2, 1, 1), (0, 1, 1), (1, 2, 1), (1, 0, 1), (1, 1, 2), (1, 1, 0)):
        first, second, third = offset
        beside = padded[:, first:first + size_x, second:second + size_y, third:third + size_z]
        visc_beside = visc_pad[first:first + size_x, second:second + size_y, third:third + size_z]
        result = result + 0.5 * (visc_mid + visc_beside) * (beside - centre)
    return result

def reference(velocity, viscosity, forcing, earlier):
    visc_pad = jnp.pad(viscosity, 1)
    field = velocity
    snapshots = []
    for index in range(STEPS):
        padded = jnp.pad(field, ((0, 0), (1, 1), (1, 1), (1, 1)))
        field = field + laplace(padded, visc_pad) + forcing[index]
        snapshots.append(field.reshape(1, -1))
    total_rows = 3 * NX * NY * NZ
    panel = jnp.concatenate([earlier.reshape(KEPT, -1)] + snapshots, 0)
    gram = lax.dot_general(panel.astype(jnp.float32), panel.astype(jnp.float32), (((1,), (1,)), ((), ())), precision=lax.Precision.HIGHEST, preferred_element_type=jnp.float32) / total_rows
    lower = jnp.linalg.cholesky(gram)
    basis = jax.scipy.linalg.solve_triangular(lower, panel, lower=True)
    return (field, basis.reshape(K, 3, NX, NY, NZ), lower.T)
```

```python
import functools
import jax
import jax.numpy as jnp
from jax import lax
from jax.experimental import pallas as pl
from jax.experimental.pallas import tpu as pltpu
from jax.sharding import PartitionSpec as P

F32 = jnp.float32
BF16 = jnp.bfloat16
DEPTH = 4
VMEM = pl.BlockSpec(memory_space=pltpu.VMEM)
PARAMS = pltpu.CompilerParams(vmem_limit_bytes=48 << 20)


def struct(*shape):
    return jax.ShapeDtypeStruct(shape, F32)


def sub_index():
    return lax.broadcasted_iota(jnp.int32, (8, 128), 0)


def turn(tile, shift):
    return pltpu.roll(tile, shift, 0)


def y_items(v, nu, f, up):
    sub = sub_index()
    comps, size_x = v.shape[0], v.shape[1]
    cells = [(c, x) for c in range(comps) for x in range(size_x)]
    items = [v[c, x] for c, x in cells] + [nu[x] for x in range(size_x)]
    for c, x in cells:
        if up:
            items.append(jnp.where(sub == 4, turn(f[2, c, x], 5), f[0, c, x]))
        else:
            items.append(jnp.where(sub == 3, turn(f[2, c, x], 3), f[0, c, x]))
    for (c, x), (d, w) in zip(cells[0::2], cells[1::2]):
        if up:
            items.append(jnp.where(sub >= 6, f[1, c, x], turn(f[1, d, w], 6)))
        else:
            items.append(jnp.where(sub < 2, f[1, c, x], turn(f[1, d, w], 2)))
    return items


def pack_y_kernel(v, nu, f, send_a, send_b):
    sub = sub_index()
    even = lax.rem(lax.axis_index("gy"), 2) == 0
    upper, lower = (y_items(v, nu, f, True), y_items(v, nu, f, False))
    half = send_a.shape[0]
    for j in range(half):
        to_up = jnp.where(sub >= 4, upper[j], turn(upper[half + j], 4))
        to_down = jnp.where(sub < 4, lower[j], turn(lower[half + j], 4))
        send_a[j] = jnp.where(even, to_up, to_down)
        send_b[j] = jnp.where(even, to_down, to_up)


def unpack_y(recv_a, recv_b, even, j):
    sub = sub_index()
    half = recv_a.shape[0]
    k = j % half
    a, b = recv_a[k], recv_b[k]
    above, below = jnp.where(even, a, b), jnp.where(even, b, a)
    if j < half:
        return jnp.where(sub < 4, above, below)
    return turn(jnp.where(sub < 4, below, above), 4)


def x_items(comps):
    own = [("v", c, d) for c in range(comps) for d in range(1, 5)]
    own += [("nu", 0, d) for d in range(1, 5)]
    for t in range(3):
        own += [(t, c, d) for c in range(comps) for d in range(1, 4 - t)]
    rim = [("v", c, d) for c in range(comps) for d in range(1, 4)]
    rim += [("nu", 0, d) for d in range(1, 4)]
    for t in range(2):
        rim += [(t, c, d) for c in range(comps) for d in range(1, 3 - t)]
    return own, rim


def pack_x_kernel(v, nu, f, recv_a, recv_b, rv, rnu, rf, send_a, send_b):
    sub = sub_index()
    even_y = lax.rem(lax.axis_index("gy"), 2) == 0
    even_x = lax.rem(lax.axis_index("gx"), 2) == 0
    comps, size_x = v.shape[0], v.shape[1]
    cells = [(c, x) for c in range(comps) for x in range(size_x)]
    get = functools.partial(unpack_y, recv_a, recv_b, even_y)
    at = 0
    for c, x in cells:
        rv[c, x] = get(at)
        at += 1
    for x in range(size_x):
        rnu[x] = get(at)
        at += 1
    for c, x in cells:
        item = get(at)
        rf[0, c, x] = item
        rf[2, c, x] = jnp.where(sub < 4, turn(item, 5), turn(item, 3))
        at += 1
    for (c, x), (d, w) in zip(cells[0::2], cells[1::2]):
        item = get(at)
        rf[1, c, x] = item
        rf[1, d, w] = jnp.where(sub < 4, turn(item, 6), turn(item, 2))
        at += 1
    own, rim = x_items(comps)
    at = 0
    for group, (gv, gnu, gf) in ((own, (v, nu, f)), (rim, (rv, rnu, rf))):
        for name, c, d in group:
            high, low = size_x - d, d - 1
            for ref, x in (
                (send_a, jnp.where(even_x, high, low)),
                (send_b, jnp.where(even_x, low, high)),
            ):
                if name == "v":
                    ref[at] = gv[c, x]
                elif name == "nu":
                    ref[at] = gnu[x]
                else:
                    ref[at] = gf[name, c, x]
            at += 1


def beside_y(first, second, up):
    sub = sub_index()
    if up:
        return jnp.where(sub == 7, turn(second, 7), turn(first, 7))
    return jnp.where(sub == 0, turn(second, 1), turn(first, 1))


def steps_kernel(v, nu, f, rv, rnu, rf, recv_a, recv_b, kept, square, snaps, final, part, ext, enu, ef, coef):
    comps, size_x = v.shape[0], v.shape[1]
    steps = f.shape[0]
    wide = 2 * size_x
    ix, nx = lax.axis_index("gx"), lax.axis_size("gx")
    iy, ny = lax.axis_index("gy"), lax.axis_size("gy")
    even = lax.rem(ix, 2) == 0
    sub = sub_index()
    lane = lax.broadcasted_iota(jnp.int32, (8, 128), 1)
    one = lambda flag: jnp.where(flag, 1.0, 0.0).astype(F32)
    x_top, x_low = one(ix < nx - 1), one(ix > 0)
    y_top, y_low = one(iy < ny - 1), one(iy > 0)

    for x in range(size_x):
        enu[x, 0], enu[x, 1] = nu[x], rnu[x]
        for c in range(comps):
            ext[0, c, x, 0], ext[0, c, x, 1] = v[c, x], rv[c, x]
            for t in range(3):
                ef[t, c, x, 0], ef[t, c, x, 1] = f[t, c, x], rf[t, c, x]
    own, rim = x_items(comps)
    at = 0
    for tile, group in enumerate((own, rim)):
        for name, c, d in group:
            high, low = size_x - 1 + d, wide - d
            for ref, x in (
                (recv_a, jnp.where(even, high, low)),
                (recv_b, jnp.where(even, low, high)),
            ):
                if name == "v":
                    ext[0, c, x, tile] = ref[at]
                elif name == "nu":
                    enu[x, tile] = ref[at]
                else:
                    ef[name, c, x, tile] = ref[at]
            at += 1

    def reach(x):
        return 0 if x < size_x else min(x - size_x + 1, wide - x)

    def tiles(limit):
        for x in range(wide):
            for tile in range(2):
                if reach(x) + tile <= limit:
                    yield x, tile

    for x, tile in tiles(DEPTH - 1):
        here, other = enu[x, tile], enu[x, 1 - tile]
        east = 0.5 * (here + enu[(x + 1) % wide, tile])
        west = 0.5 * (here + enu[(x - 1) % wide, tile])
        north = 0.5 * (here + beside_y(here, other, True))
        south = 0.5 * (here + beside_y(here, other, False))
        ahead = jnp.where(lane == 127, 0.0, pltpu.roll(here, 127, 1))
        behind = jnp.where(lane == 0, 0.0, pltpu.roll(here, 1, 1))
        front = 0.5 * (here + ahead)
        back = 0.5 * (here + behind)
        coef[x, tile, 0] = 1.0 - (((east + west) + (north + south)) + (front + back))
        if x == size_x - 1:
            east = east * x_top
        if x == 0:
            west = west * x_low
        if tile == 0:
            north = jnp.where(sub == 7, north * y_top, north)
            south = jnp.where(sub == 0, south * y_low, south)
        coef[x, tile, 1], coef[x, tile, 2] = east, west
        coef[x, tile, 3], coef[x, tile, 4] = north, south
        coef[x, tile, 5] = jnp.where(lane == 127, 0.0, front)
        coef[x, tile, 6] = jnp.where(lane == 0, 0.0, back)

    for t in range(steps):
        src, dst = t % 2, (t + 1) % 2
        for x, tile in tiles(DEPTH - 1 - t):
            w = [coef[x, tile, i] for i in range(7)]
            for c in range(comps):
                here, other = ext[src, c, x, tile], ext[src, c, x, 1 - tile]
                new = w[0] * here
                new = new + w[1] * ext[src, c, (x + 1) % wide, tile]
                new = new + w[2] * ext[src, c, (x - 1) % wide, tile]
                new = new + w[3] * beside_y(here, other, True)
                new = new + w[4] * beside_y(here, other, False)
                new = new + w[5] * pltpu.roll(here, 127, 1)
                new = new + w[6] * pltpu.roll(here, 1, 1)
                push = ef[t, c, x, tile] if t < 3 else f[t, c, x]
                new = new + push
                if t < steps - 1:
                    ext[dst, c, x, tile] = new
                if tile == 0 and x < size_x:
                    snaps[t, c * size_x + x] = new
                    if t == steps - 1:
                        final[c, x] = new

    rows = kept.shape[0]
    slabs = kept.shape[1]
    n = rows + steps
    column = lax.broadcasted_iota(jnp.int32, (8, n), 1)
    total = square[...]
    old = 0.5 * total[:, :n] + total[:, n:]
    scale = 1.0 / (slabs * 8 * 128 * nx * ny)
    for k0 in range(0, n, 8):
        acc = [[None] * 8 for _ in range(steps)]
        for s in range(slabs):
            new = [snaps[t, s] for t in range(steps)]
            for k in range(8):
                row = kept[k0 + k, s] if k0 + k < rows else new[k0 + k - rows]
                for t in range(steps):
                    if k0 + k >= rows and k0 + k - rows > t:
                        continue
                    term = row * new[t]
                    acc[t][k] = term if acc[t][k] is None else acc[t][k] + term
        block = old[k0 : k0 + 8]
        for t in range(steps):
            full = jnp.stack([jnp.zeros((8, 128), F32) if a is None else a for a in acc[t]], 0)
            summed = jnp.sum(pltpu.einshape("kyz->ykz", full), axis=0)
            entry = jnp.sum(summed, axis=1, keepdims=True)
            if k0 + 8 > rows:
                row_at = lax.broadcasted_iota(jnp.int32, (8, 1), 0) + k0
                entry = jnp.where(row_at == rows + t, 0.5 * entry, entry)
            block = jnp.where(column == rows + t, entry, block)
        part[pl.ds(k0, 8), :] = block * scale


def split(p):
    high = p.astype(BF16)
    return high, (p - high.astype(F32)).astype(BF16)


def to_rows(tiles):
    parts = [pltpu.einshape("kyz->ykz", tiles[k : k + 8]) for k in range(0, tiles.shape[0], 8)]
    return [jnp.concatenate([p[y] for p in parts], 0) for y in range(8)]


def from_rows(rows):
    n = rows[0].shape[0]
    return jnp.concatenate(
        [
            pltpu.einshape("ykz->kyz", jnp.stack([r[k : k + 8] for r in rows], 0))
            for k in range(0, n, 8)
        ],
        0,
    )


def square_kernel(kept, out, *, n):
    rows, slabs = kept.shape[0], kept.shape[1]
    acc = None
    for s in range(slabs):
        tiles = jnp.concatenate([kept[:, s], jnp.zeros((n - rows, 8, 128), F32)], 0)
        lines = to_rows(tiles)
        for y in range(0, 8, 2):
            high, low = split(jnp.concatenate(lines[y : y + 2], 1))
            both = jnp.concatenate([high, low], 0)
            term = lax.dot_general(high, both, (((1,), (1,)), ((), ())), preferred_element_type=F32)
            acc = term if acc is None else acc + term
    out[...] = acc


def factor_of(gram):
    n = gram.shape[0]
    row_at = lax.broadcasted_iota(jnp.int32, (n, n), 0)
    col_at = lax.broadcasted_iota(jnp.int32, (n, n), 1)
    eye = jnp.where(row_at == col_at, 1.0, 0.0).astype(F32)
    w = jnp.concatenate([gram, eye], 1)
    at = lax.broadcasted_iota(jnp.int32, (n, 1), 0)
    for j in range(n - 1):
        row = w[j : j + 1, :]
        ratio = row * (1.0 / row[:, j : j + 1])
        w = w - jnp.where(at > j, w[:, j : j + 1], 0.0) * ratio
    pivot = jnp.sum(w[:, :n] * eye, axis=1, keepdims=True)
    return w * lax.rsqrt(pivot)


def basis_kernel(part, kept, snaps, basis, factor, left):
    n = part.shape[0]
    block = basis.shape[1]

    @pl.when(pl.program_id(0) == 0)
    def _():
        m = part[...]
        w = factor_of(m + m.T)
        row_at = lax.broadcasted_iota(jnp.int32, (n, n), 0)
        col_at = lax.broadcasted_iota(jnp.int32, (n, n), 1)
        factor[...] = jnp.where(row_at <= col_at, w[:, :n], 0.0)
        high, low = split(w[:, n:])
        top = jnp.concatenate([high, high], 1)
        left[...] = jnp.concatenate([top, jnp.concatenate([low, jnp.zeros_like(low)], 1)], 0)

    lhs = left[...]
    base = pl.program_id(0) * block
    for s in range(block):
        lines = to_rows(jnp.concatenate([kept[:, base + s], snaps[:, base + s]], 0))
        out = []
        for y in range(0, 8, 2):
            high, low = split(jnp.concatenate(lines[y : y + 2], 1))
            rhs = jnp.concatenate([high, low], 0)
            r = lax.dot_general(lhs, rhs, (((1,), (0,)), ((), ())), preferred_element_type=F32)
            r = r[:n] + r[n:]
            out += [r[:, :128], r[:, 128:]]
        basis[:, s] = from_rows(out)


def pair_exchange(first, second, axis):
    count = lax.axis_size(axis)
    near = [(i, i ^ 1) for i in range(count)]
    far = [(i, ((i + 1) ^ 1) - 1) for i in range(1, count - 1)]
    return lax.ppermute(first, axis, near), lax.ppermute(second, axis, far)


def sum_over(value, axes):
    sizes = [lax.axis_size(a) for a in axes]
    count = 1
    for size in sizes:
        count *= size
    bits = []
    bit = 1
    while bit < count:
        bits.append(bit)
        bit *= 2
    for bit in reversed(bits):
        value = value + lax.ppermute(value, axes, [(i, i ^ bit) for i in range(count)])
    return value


def local(velocity, viscosity, forcing, earlier):
    comps, size_x = velocity.shape[0], velocity.shape[1]
    steps, rows = forcing.shape[0], earlier.shape[0]
    n, slabs = rows + steps, comps * size_x
    kept = earlier.reshape(rows, slabs, 8, 128)
    half = (2 * slabs + size_x + slabs // 2) // 2
    call = functools.partial(pl.pallas_call, compiler_params=PARAMS)
    send_a, send_b = call(
        pack_y_kernel,
        out_shape=(struct(half, 8, 128),) * 2,
        in_specs=[VMEM] * 3,
        out_specs=(VMEM,) * 2,
        name="pack_y",
    )(velocity, viscosity, forcing)
    recv_a, recv_b = pair_exchange(send_a, send_b, "gy")
    square = call(
        functools.partial(square_kernel, n=n),
        out_shape=struct(n, 2 * n),
        in_specs=[VMEM],
        out_specs=VMEM,
        cost_estimate=pl.CostEstimate(flops=2 * n * 2 * n * slabs * 1024, transcendentals=0, bytes_accessed=rows * slabs * 4096 * 2),
        name="gram_kept",
    )(kept)
    own, rim = x_items(comps)
    wire = struct(len(own) + len(rim), 8, 128)
    rv, rnu, rf, send_a, send_b = call(
        pack_x_kernel,
        out_shape=(
            struct(*velocity.shape),
            struct(*viscosity.shape),
            struct(3, *velocity.shape),
            wire,
            wire,
        ),
        in_specs=[VMEM] * 5,
        out_specs=(VMEM,) * 5,
        name="pack_x",
    )(velocity, viscosity, forcing, recv_a, recv_b)
    recv_a, recv_b = pair_exchange(send_a, send_b, "gx")
    snaps, final, part = call(
        steps_kernel,
        out_shape=(struct(steps, slabs, 8, 128), struct(*velocity.shape), struct(n, n)),
        in_specs=[VMEM] * 10,
        out_specs=(VMEM,) * 3,
        scratch_shapes=[
            pltpu.VMEM((2, comps, 2 * size_x, 2, 8, 128), F32),
            pltpu.VMEM((2 * size_x, 2, 8, 128), F32),
            pltpu.VMEM((3, comps, 2 * size_x, 2, 8, 128), F32),
            pltpu.VMEM((2 * size_x, 2, 7, 8, 128), F32),
        ],
        name="steps",
    )(velocity, viscosity, forcing, rv, rnu, rf, recv_a, recv_b, kept, square)
    part = sum_over(part, ("gx", "gy"))
    block = 6
    basis, factor = call(
        basis_kernel,
        grid=(slabs // block,),
        out_shape=(struct(n, slabs, 8, 128), struct(n, n)),
        in_specs=[VMEM] * 3,
        out_specs=(
            pl.BlockSpec((n, block, 8, 128), lambda i: (0, i, 0, 0)),
            pl.BlockSpec((n, n), lambda i: (0, 0)),
        ),
        scratch_shapes=[pltpu.VMEM((2 * n, 2 * n), BF16)],
        name="factor_basis",
    )(part, kept, snaps)
    return final, basis.reshape((n,) + velocity.shape), factor


def solution(mesh):
    return jax.shard_map(
        local,
        mesh=mesh,
        in_specs=(
            P(None, "gx", "gy", None),
            P("gx", "gy", None),
            P(None, None, "gx", "gy", None),
            P(None, None, "gx", "gy", None),
        ),
        out_specs=(P(None, "gx", "gy", None), P(None, None, "gx", "gy", None), P()),
        check_vma=False,
    )
```

```python
import functools
import jax
import jax.numpy as jnp
from jax import lax
from jax.experimental import pallas as pl
from jax.experimental.pallas import tpu as pltpu
from jax.sharding import PartitionSpec as P

F32 = jnp.float32
BF16 = jnp.bfloat16
DEPTH = 4
VMEM = pl.BlockSpec(memory_space=pltpu.VMEM)
HBM = pl.BlockSpec(memory_space=pltpu.HBM)


def limit(mib):
    return pltpu.CompilerParams(vmem_limit_bytes=mib << 20)


def struct(*shape):
    return jax.ShapeDtypeStruct(shape, F32)


def sub_index():
    return lax.broadcasted_iota(jnp.int32, (8, 128), 0)


def turn(tile, shift):
    return pltpu.roll(tile, shift, 0)


def y_items(v, nu, f, up):
    sub = sub_index()
    comps, size_x = v.shape[0], v.shape[1]
    cells = [(c, x) for c in range(comps) for x in range(size_x)]
    items = [v[c, x] for c, x in cells] + [nu[x] for x in range(size_x)]
    for c, x in cells:
        if up:
            items.append(jnp.where(sub == 4, turn(f[2, c, x], 5), f[0, c, x]))
        else:
            items.append(jnp.where(sub == 3, turn(f[2, c, x], 3), f[0, c, x]))
    for (c, x), (d, w) in zip(cells[0::2], cells[1::2]):
        if up:
            items.append(jnp.where(sub >= 6, f[1, c, x], turn(f[1, d, w], 6)))
        else:
            items.append(jnp.where(sub < 2, f[1, c, x], turn(f[1, d, w], 2)))
    return items


def pack_y_kernel(v_in, nu_in, f_in, v, nu, f, send_a, send_b, sems):
    pairs = ((f_in, f), (v_in, v), (nu_in, nu))
    copies = [pltpu.make_async_copy(a, b, sems.at[i]) for i, (a, b) in enumerate(pairs)]
    for copy in copies:
        copy.start()
    for copy in copies:
        copy.wait()
    sub = sub_index()
    even = lax.rem(lax.axis_index("gy"), 2) == 0
    upper, lower = (y_items(v, nu, f, True), y_items(v, nu, f, False))
    half = send_a.shape[0]
    for j in range(half):
        to_up = jnp.where(sub >= 4, upper[j], turn(upper[half + j], 4))
        to_down = jnp.where(sub < 4, lower[j], turn(lower[half + j], 4))
        send_a[j] = jnp.where(even, to_up, to_down)
        send_b[j] = jnp.where(even, to_down, to_up)


def unpack_y(recv_a, recv_b, even, j):
    sub = sub_index()
    half = recv_a.shape[0]
    k = j % half
    a, b = recv_a[k], recv_b[k]
    above, below = jnp.where(even, a, b), jnp.where(even, b, a)
    if j < half:
        return jnp.where(sub < 4, above, below)
    return turn(jnp.where(sub < 4, below, above), 4)


def x_items(comps):
    own = [("v", c, d) for c in range(comps) for d in range(1, 5)]
    own += [("nu", 0, d) for d in range(1, 5)]
    for t in range(3):
        own += [(t, c, d) for c in range(comps) for d in range(1, 4 - t)]
    rim = [("v", c, d) for c in range(comps) for d in range(1, 4)]
    rim += [("nu", 0, d) for d in range(1, 4)]
    for t in range(2):
        rim += [(t, c, d) for c in range(comps) for d in range(1, 3 - t)]
    return own, rim


def pack_x_kernel(v, nu, f, recv_a, recv_b, after, rv, rnu, rf, send_a, send_b):
    sub = sub_index()
    even_y = lax.rem(lax.axis_index("gy"), 2) == 0
    even_x = lax.rem(lax.axis_index("gx"), 2) == 0
    comps, size_x = v.shape[0], v.shape[1]
    cells = [(c, x) for c in range(comps) for x in range(size_x)]
    get = functools.partial(unpack_y, recv_a, recv_b, even_y)
    at = 0
    for c, x in cells:
        rv[c, x] = get(at)
        at += 1
    for x in range(size_x):
        rnu[x] = get(at)
        at += 1
    for c, x in cells:
        item = get(at)
        rf[0, c, x] = item
        rf[2, c, x] = jnp.where(sub < 4, turn(item, 5), turn(item, 3))
        at += 1
    for (c, x), (d, w) in zip(cells[0::2], cells[1::2]):
        item = get(at)
        rf[1, c, x] = item
        rf[1, d, w] = jnp.where(sub < 4, turn(item, 6), turn(item, 2))
        at += 1
    own, rim = x_items(comps)
    at = 0
    for group, (gv, gnu, gf) in ((own, (v, nu, f)), (rim, (rv, rnu, rf))):
        for name, c, d in group:
            high, low = size_x - d, d - 1
            for ref, x in (
                (send_a, jnp.where(even_x, high, low)),
                (send_b, jnp.where(even_x, low, high)),
            ):
                if name == "v":
                    ref[at] = gv[c, x]
                elif name == "nu":
                    ref[at] = gnu[x]
                else:
                    ref[at] = gf[name, c, x]
            at += 1


def beside_y(first, second, up):
    sub = sub_index()
    if up:
        return jnp.where(sub == 7, turn(second, 7), turn(first, 7))
    return jnp.where(sub == 0, turn(second, 1), turn(first, 1))


def steps_kernel(v, nu, f, rv, rnu, rf, recv_a, recv_b, kept, square_a, square_b, snaps, final, part, ext, enu, ef, coef):
    comps, size_x = v.shape[0], v.shape[1]
    steps = f.shape[0]
    wide = 2 * size_x
    ix, nx = lax.axis_index("gx"), lax.axis_size("gx")
    iy, ny = lax.axis_index("gy"), lax.axis_size("gy")
    even = lax.rem(ix, 2) == 0
    sub = sub_index()
    lane = lax.broadcasted_iota(jnp.int32, (8, 128), 1)
    one = lambda flag: jnp.where(flag, 1.0, 0.0).astype(F32)
    x_top, x_low = one(ix < nx - 1), one(ix > 0)
    y_top, y_low = one(iy < ny - 1), one(iy > 0)

    for x in range(size_x):
        enu[x, 0], enu[x, 1] = nu[x], rnu[x]
        for c in range(comps):
            ext[0, c, x, 0], ext[0, c, x, 1] = v[c, x], rv[c, x]
            for t in range(3):
                ef[t, c, x, 0], ef[t, c, x, 1] = f[t, c, x], rf[t, c, x]
    own, rim = x_items(comps)
    at = 0
    for tile, group in enumerate((own, rim)):
        for name, c, d in group:
            high, low = size_x - 1 + d, wide - d
            for ref, x in (
                (recv_a, jnp.where(even, high, low)),
                (recv_b, jnp.where(even, low, high)),
            ):
                if name == "v":
                    ext[0, c, x, tile] = ref[at]
                elif name == "nu":
                    enu[x, tile] = ref[at]
                else:
                    ef[name, c, x, tile] = ref[at]
            at += 1

    def reach(x):
        return 0 if x < size_x else min(x - size_x + 1, wide - x)

    def tiles(limit):
        for x in range(wide):
            for tile in range(2):
                if reach(x) + tile <= limit:
                    yield x, tile

    for x, tile in tiles(DEPTH - 1):
        here, other = enu[x, tile], enu[x, 1 - tile]
        east = 0.5 * (here + enu[(x + 1) % wide, tile])
        west = 0.5 * (here + enu[(x - 1) % wide, tile])
        north = 0.5 * (here + beside_y(here, other, True))
        south = 0.5 * (here + beside_y(here, other, False))
        ahead = jnp.where(lane == 127, 0.0, pltpu.roll(here, 127, 1))
        behind = jnp.where(lane == 0, 0.0, pltpu.roll(here, 1, 1))
        front = 0.5 * (here + ahead)
        back = 0.5 * (here + behind)
        coef[x, tile, 0] = 1.0 - (((east + west) + (north + south)) + (front + back))
        if x == size_x - 1:
            east = east * x_top
        if x == 0:
            west = west * x_low
        if tile == 0:
            north = jnp.where(sub == 7, north * y_top, north)
            south = jnp.where(sub == 0, south * y_low, south)
        coef[x, tile, 1], coef[x, tile, 2] = east, west
        coef[x, tile, 3], coef[x, tile, 4] = north, south
        coef[x, tile, 5] = jnp.where(lane == 127, 0.0, front)
        coef[x, tile, 6] = jnp.where(lane == 0, 0.0, back)

    for t in range(steps):
        src, dst = t % 2, (t + 1) % 2
        for x, tile in tiles(DEPTH - 1 - t):
            w = [coef[x, tile, i] for i in range(7)]
            for c in range(comps):
                here, other = ext[src, c, x, tile], ext[src, c, x, 1 - tile]
                new = w[0] * here
                new = new + w[1] * ext[src, c, (x + 1) % wide, tile]
                new = new + w[2] * ext[src, c, (x - 1) % wide, tile]
                new = new + w[3] * beside_y(here, other, True)
                new = new + w[4] * beside_y(here, other, False)
                new = new + w[5] * pltpu.roll(here, 127, 1)
                new = new + w[6] * pltpu.roll(here, 1, 1)
                push = ef[t, c, x, tile] if t < 3 else f[t, c, x]
                new = new + push
                if t < steps - 1:
                    ext[dst, c, x, tile] = new
                if tile == 0 and x < size_x:
                    snaps[t, c * size_x + x] = new
                    if t == steps - 1:
                        final[c, x] = new

    rows = kept.shape[0]
    slabs = kept.shape[1]
    n = rows + steps
    column = lax.broadcasted_iota(jnp.int32, (8, n), 1)
    total = square_a[...] + square_b[...]
    old = 0.5 * total[:, :n] + total[:, n:]
    scale = 1.0 / (slabs * 8 * 128 * nx * ny)
    for k0 in range(0, n, 8):
        acc = [[None] * 8 for _ in range(steps)]
        for s in range(slabs):
            new = [snaps[t, s] for t in range(steps)]
            for k in range(8):
                row = kept[k0 + k, s] if k0 + k < rows else new[k0 + k - rows]
                for t in range(steps):
                    if k0 + k >= rows and k0 + k - rows > t:
                        continue
                    term = row * new[t]
                    acc[t][k] = term if acc[t][k] is None else acc[t][k] + term
        block = old[k0 : k0 + 8]
        for t in range(steps):
            full = jnp.stack([jnp.zeros((8, 128), F32) if a is None else a for a in acc[t]], 0)
            summed = jnp.sum(pltpu.einshape("kyz->ykz", full), axis=0)
            entry = jnp.sum(summed, axis=1, keepdims=True)
            if k0 + 8 > rows:
                row_at = lax.broadcasted_iota(jnp.int32, (8, 1), 0) + k0
                entry = jnp.where(row_at == rows + t, 0.5 * entry, entry)
            block = jnp.where(column == rows + t, entry, block)
        part[pl.ds(k0, 8), :] = block * scale


def split(p):
    high = p.astype(BF16)
    return high, (p - high.astype(F32)).astype(BF16)


def to_rows(tiles):
    parts = [pltpu.einshape("kyz->ykz", tiles[k : k + 8]) for k in range(0, tiles.shape[0], 8)]
    return [jnp.concatenate([p[y] for p in parts], 0) for y in range(8)]


def from_rows(rows):
    n = rows[0].shape[0]
    return jnp.concatenate(
        [
            pltpu.einshape("ykz->kyz", jnp.stack([r[k : k + 8] for r in rows], 0))
            for k in range(0, n, 8)
        ],
        0,
    )


def square_of(kept, slabs, n, ready=None):
    rows = kept.shape[0]
    acc = None
    for s in slabs:
        if ready is not None:
            ready(s)
        tiles = jnp.concatenate([kept[:, s], jnp.zeros((n - rows, 8, 128), F32)], 0)
        lines = to_rows(tiles)
        for y in range(0, 8, 2):
            high, low = split(jnp.concatenate(lines[y : y + 2], 1))
            both = jnp.concatenate([high, low], 0)
            term = lax.dot_general(high, both, (((1,), (1,)), ((), ())), preferred_element_type=F32)
            acc = term if acc is None else acc + term
    return acc


def square_first_kernel(kept_in, kept, out, sems, *, n, count):
    slabs = kept.shape[1]
    step = slabs // sems.shape[0]
    copies = []
    for i in range(sems.shape[0]):
        at = (slice(None), pl.ds(i * step, step))
        copies.append(pltpu.make_async_copy(kept_in.at[at], kept.at[at], sems.at[i]))
    for copy in copies:
        copy.start()

    def ready(s):
        if s % step == 0:
            copies[s // step].wait()

    out[...] = square_of(kept, range(count), n, ready)
    for i in range(-(-count // step), len(copies)):
        copies[i].wait()


def square_rest_kernel(kept, out, *, n, count):
    out[...] = square_of(kept, range(count, kept.shape[1]), n)


def factor_of(gram):
    n = gram.shape[0]
    count = n // 8
    sub = sub_index()
    row_at = lax.broadcasted_iota(jnp.int32, (n, n), 0)
    col_at = lax.broadcasted_iota(jnp.int32, (n, n), 1)
    eye = jnp.where(row_at == col_at, 1.0, 0.0).astype(F32)
    whole = jnp.concatenate([gram, eye], 1)
    w = [whole[8 * c : 8 * c + 8] for c in range(count)]

    def spread(tile, j):
        return jnp.broadcast_to(tile[:, j : j + 1], tile.shape)

    def pick(tile, q):
        return jnp.broadcast_to(tile[q : q + 1, :], tile.shape)

    for b in range(count):
        cols = {c: [spread(w[c], 8 * b + q) for q in range(8)] for c in range(b, count)}
        pivots = jnp.ones(w[b].shape, F32)
        for q in range(8):
            head = [pick(cols[b][r], q) for r in range(q, 8)]
            inverse = 1.0 / head[0]
            pivots = jnp.where(sub == q, head[0], pivots)
            line = pick(w[b], q)
            for c in range(b, count):
                ratio = cols[c][q] * inverse
                if c == b:
                    ratio = jnp.where(sub > q, ratio, 0.0)
                w[c] = w[c] - ratio * line
                for r in range(q + 1, 8):
                    cols[c][r] = cols[c][r] - ratio * head[r - q]
        w[b] = w[b] * lax.rsqrt(pivots)
    return jnp.concatenate(w, 0)


def basis_kernel(part, kept, snaps, basis, factor, out, sems):
    n = part.shape[0]
    slabs = kept.shape[1]
    block = slabs // sems.shape[0]
    m = part[...]
    w = factor_of(m + m.T)
    row_at = lax.broadcasted_iota(jnp.int32, (n, n), 0)
    col_at = lax.broadcasted_iota(jnp.int32, (n, n), 1)
    factor[...] = jnp.where(row_at <= col_at, w[:, :n], 0.0)
    high, low = split(w[:, n:])
    lhs = jnp.concatenate([high, high, low], 1)
    copies = []
    for s in range(slabs):
        lines = to_rows(jnp.concatenate([kept[:, s], snaps[:, s]], 0))
        pieces = []
        for y in range(0, 8, 2):
            high, low = split(jnp.concatenate(lines[y : y + 2], 1))
            rhs = jnp.concatenate([high, low, high], 0)
            r = lax.dot_general(lhs, rhs, (((1,), (0,)), ((), ())), preferred_element_type=F32)
            pieces += [r[:, :128], r[:, 128:]]
        out[:, s] = from_rows(pieces)
        if (s + 1) % block == 0:
            at = (slice(None), pl.ds(s + 1 - block, block))
            copy = pltpu.make_async_copy(out.at[at], basis.at[at], sems.at[s // block])
            copy.start()
            copies.append(copy)
    for copy in copies:
        copy.wait()


def pair_exchange(first, second, axis):
    count = lax.axis_size(axis)
    near = [(i, i ^ 1) for i in range(count)]
    far = [(i, ((i + 1) ^ 1) - 1) for i in range(1, count - 1)]
    distant = lax.ppermute(second, axis, far)
    return lax.ppermute(first, axis, near), distant


def sum_over(value, axes):
    count = 1
    for axis in axes:
        count *= lax.axis_size(axis)
    bits = []
    while 2 ** len(bits) < count:
        bits.append(2 ** len(bits))
    bits = bits[::-1]
    for group in [bits[i : i + 2] for i in range(0, len(bits), 2)]:
        masks = group + ([group[0] ^ group[1]] if len(group) == 2 else [])
        others = [lax.ppermute(value, axes, [(i, i ^ m) for i in range(count)]) for m in masks]
        for other in others:
            value = value + other
    return value


def local(velocity, viscosity, forcing, earlier):
    comps, size_x = velocity.shape[0], velocity.shape[1]
    steps, rows = forcing.shape[0], earlier.shape[0]
    n, slabs = rows + steps, comps * size_x
    half = (2 * slabs + size_x + slabs // 2) // 2
    call = pl.pallas_call
    v, nu, f, send_a, send_b = call(
        pack_y_kernel,
        out_shape=(
            struct(*velocity.shape),
            struct(*viscosity.shape),
            struct(*forcing.shape),
            struct(half, 8, 128),
            struct(half, 8, 128),
        ),
        in_specs=[HBM] * 3,
        out_specs=(VMEM,) * 5,
        scratch_shapes=[pltpu.SemaphoreType.DMA((3,))],
        compiler_params=limit(8),
        name="pack_y",
    )(*[pltpu.with_memory_space_constraint(a, pltpu.HBM) for a in (velocity, viscosity, forcing)])
    recv_a, recv_b = pair_exchange(send_a, send_b, "gy")
    first = slabs * 2 // 3
    kept, square_a = call(
        functools.partial(square_first_kernel, n=n, count=first),
        out_shape=(struct(rows, slabs, 8, 128), struct(n, 2 * n)),
        in_specs=[HBM],
        out_specs=(VMEM,) * 2,
        scratch_shapes=[pltpu.SemaphoreType.DMA((6,))],
        compiler_params=limit(8),
        name="gram_first",
    )(pltpu.with_memory_space_constraint(earlier.reshape(rows, slabs, 8, 128), pltpu.HBM))
    own, rim = x_items(comps)
    wire = struct(len(own) + len(rim), 8, 128)
    rv, rnu, rf, send_a, send_b = call(
        pack_x_kernel,
        out_shape=(
            struct(*velocity.shape),
            struct(*viscosity.shape),
            struct(3, *velocity.shape),
            wire,
            wire,
        ),
        in_specs=[VMEM] * 5 + [pl.BlockSpec(memory_space=pl.ANY)],
        out_specs=(VMEM,) * 5,
        compiler_params=limit(8),
        name="pack_x",
    )(v, nu, f, recv_a, recv_b, square_a)
    recv_a, recv_b = pair_exchange(send_a, send_b, "gx")
    square_b = call(
        functools.partial(square_rest_kernel, n=n, count=first),
        out_shape=struct(n, 2 * n),
        in_specs=[VMEM],
        out_specs=VMEM,
        compiler_params=limit(8),
        name="gram_rest",
    )(kept)
    snaps, final, part = call(
        steps_kernel,
        out_shape=(struct(steps, slabs, 8, 128), struct(*velocity.shape), struct(n, n)),
        in_specs=[VMEM] * 11,
        out_specs=(VMEM,) * 3,
        scratch_shapes=[
            pltpu.VMEM((2, comps, 2 * size_x, 2, 8, 128), F32),
            pltpu.VMEM((2 * size_x, 2, 8, 128), F32),
            pltpu.VMEM((3, comps, 2 * size_x, 2, 8, 128), F32),
            pltpu.VMEM((2 * size_x, 2, 7, 8, 128), F32),
        ],
        compiler_params=limit(12),
        name="steps",
    )(v, nu, f, rv, rnu, rf, recv_a, recv_b, kept, square_a, square_b)
    part = sum_over(part, ("gx", "gy"))
    basis, factor = call(
        basis_kernel,
        out_shape=(struct(n, slabs, 8, 128), struct(n, n)),
        in_specs=[VMEM] * 3,
        out_specs=(HBM, VMEM),
        scratch_shapes=[pltpu.VMEM((n, slabs, 8, 128), F32), pltpu.SemaphoreType.DMA((slabs // 3,))],
        compiler_params=limit(16),
        name="factor_basis",
    )(part, kept, snaps)
    return final, basis.reshape((n,) + velocity.shape), factor


def solution(mesh):
    return jax.shard_map(
        local,
        mesh=mesh,
        in_specs=(
            P(None, "gx", "gy", None),
            P("gx", "gy", None),
            P(None, None, "gx", "gy", None),
            P(None, None, "gx", "gy", None),
        ),
        out_specs=(P(None, "gx", "gy", None), P(None, None, "gx", "gy", None), P()),
        check_vma=False,
    )
```

```python
import functools
import jax
import jax.numpy as jnp
from jax import lax
from jax.experimental import pallas as pl
from jax.experimental.pallas import tpu as pltpu
from jax.sharding import PartitionSpec as P

F32 = jnp.float32
BF16 = jnp.bfloat16
DEPTH = 4
VMEM = pl.BlockSpec(memory_space=pltpu.VMEM)
HBM = pl.BlockSpec(memory_space=pltpu.HBM)


def limit(mib):
    return pltpu.CompilerParams(vmem_limit_bytes=mib << 20)


def struct(*shape):
    return jax.ShapeDtypeStruct(shape, F32)


def sub_index():
    return lax.broadcasted_iota(jnp.int32, (8, 128), 0)


def turn(tile, shift):
    return pltpu.roll(tile, shift, 0)


def y_items(v, nu, f, up):
    sub = sub_index()
    comps, size_x = v.shape[0], v.shape[1]
    cells = [(c, x) for c in range(comps) for x in range(size_x)]
    items = [v[c, x] for c, x in cells] + [nu[x] for x in range(size_x)]
    for c, x in cells:
        if up:
            items.append(jnp.where(sub == 4, turn(f[2, c, x], 5), f[0, c, x]))
        else:
            items.append(jnp.where(sub == 3, turn(f[2, c, x], 3), f[0, c, x]))
    for (c, x), (d, w) in zip(cells[0::2], cells[1::2]):
        if up:
            items.append(jnp.where(sub >= 6, f[1, c, x], turn(f[1, d, w], 6)))
        else:
            items.append(jnp.where(sub < 2, f[1, c, x], turn(f[1, d, w], 2)))
    return items


def pack_y_kernel(v_in, nu_in, f_in, v, nu, f, send_a, send_b, sems):
    pairs = ((f_in, f), (v_in, v), (nu_in, nu))
    copies = [pltpu.make_async_copy(a, b, sems.at[i]) for i, (a, b) in enumerate(pairs)]
    for copy in copies:
        copy.start()
    for copy in copies:
        copy.wait()
    sub = sub_index()
    even = lax.rem(lax.axis_index("gy"), 2) == 0
    upper, lower = (y_items(v, nu, f, True), y_items(v, nu, f, False))
    half = send_a.shape[0]
    for j in range(half):
        to_up = jnp.where(sub >= 4, upper[j], turn(upper[half + j], 4))
        to_down = jnp.where(sub < 4, lower[j], turn(lower[half + j], 4))
        send_a[j] = jnp.where(even, to_up, to_down)
        send_b[j] = jnp.where(even, to_down, to_up)


def unpack_y(recv_a, recv_b, even, j):
    sub = sub_index()
    half = recv_a.shape[0]
    k = j % half
    a, b = recv_a[k], recv_b[k]
    above, below = jnp.where(even, a, b), jnp.where(even, b, a)
    if j < half:
        return jnp.where(sub < 4, above, below)
    return turn(jnp.where(sub < 4, below, above), 4)


def x_items(comps):
    own = [("v", c, d) for c in range(comps) for d in range(1, 5)]
    own += [("nu", 0, d) for d in range(1, 5)]
    for t in range(3):
        own += [(t, c, d) for c in range(comps) for d in range(1, 4 - t)]
    rim = [("v", c, d) for c in range(comps) for d in range(1, 4)]
    rim += [("nu", 0, d) for d in range(1, 4)]
    for t in range(2):
        rim += [(t, c, d) for c in range(comps) for d in range(1, 3 - t)]
    return own, rim


def pack_x_kernel(v, nu, f, recv_a, recv_b, after, rv, rnu, rf, send_a, send_b):
    sub = sub_index()
    even_y = lax.rem(lax.axis_index("gy"), 2) == 0
    even_x = lax.rem(lax.axis_index("gx"), 2) == 0
    comps, size_x = v.shape[0], v.shape[1]
    cells = [(c, x) for c in range(comps) for x in range(size_x)]
    get = functools.partial(unpack_y, recv_a, recv_b, even_y)
    at = 0
    for c, x in cells:
        rv[c, x] = get(at)
        at += 1
    for x in range(size_x):
        rnu[x] = get(at)
        at += 1
    for c, x in cells:
        item = get(at)
        rf[0, c, x] = item
        rf[2, c, x] = jnp.where(sub < 4, turn(item, 5), turn(item, 3))
        at += 1
    for (c, x), (d, w) in zip(cells[0::2], cells[1::2]):
        item = get(at)
        rf[1, c, x] = item
        rf[1, d, w] = jnp.where(sub < 4, turn(item, 6), turn(item, 2))
        at += 1
    own, rim = x_items(comps)
    at = 0
    for group, (gv, gnu, gf) in ((own, (v, nu, f)), (rim, (rv, rnu, rf))):
        for name, c, d in group:
            high, low = size_x - d, d - 1
            for ref, x in (
                (send_a, jnp.where(even_x, high, low)),
                (send_b, jnp.where(even_x, low, high)),
            ):
                if name == "v":
                    ref[at] = gv[c, x]
                elif name == "nu":
                    ref[at] = gnu[x]
                else:
                    ref[at] = gf[name, c, x]
            at += 1


def beside_y(first, second, up):
    sub = sub_index()
    if up:
        return jnp.where(sub == 7, turn(second, 7), turn(first, 7))
    return jnp.where(sub == 0, turn(second, 1), turn(first, 1))


def steps_kernel(v, nu, f, rv, rnu, rf, recv_a, recv_b, kept, square_a, square_b, snaps, final, part, ext, enu, ef, coef):
    comps, size_x = v.shape[0], v.shape[1]
    steps = f.shape[0]
    wide = 2 * size_x
    ix, nx = lax.axis_index("gx"), lax.axis_size("gx")
    iy, ny = lax.axis_index("gy"), lax.axis_size("gy")
    even = lax.rem(ix, 2) == 0
    sub = sub_index()
    lane = lax.broadcasted_iota(jnp.int32, (8, 128), 1)
    one = lambda flag: jnp.where(flag, 1.0, 0.0).astype(F32)
    x_top, x_low = one(ix < nx - 1), one(ix > 0)
    y_top, y_low = one(iy < ny - 1), one(iy > 0)

    for x in range(size_x):
        enu[x, 0], enu[x, 1] = nu[x], rnu[x]
        for c in range(comps):
            ext[0, c, x, 0], ext[0, c, x, 1] = v[c, x], rv[c, x]
            for t in range(3):
                ef[t, c, x, 0], ef[t, c, x, 1] = f[t, c, x], rf[t, c, x]
    own, rim = x_items(comps)
    at = 0
    for tile, group in enumerate((own, rim)):
        for name, c, d in group:
            high, low = size_x - 1 + d, wide - d
            for ref, x in (
                (recv_a, jnp.where(even, high, low)),
                (recv_b, jnp.where(even, low, high)),
            ):
                if name == "v":
                    ext[0, c, x, tile] = ref[at]
                elif name == "nu":
                    enu[x, tile] = ref[at]
                else:
                    ef[name, c, x, tile] = ref[at]
            at += 1

    def reach(x):
        return 0 if x < size_x else min(x - size_x + 1, wide - x)

    def tiles(limit):
        for x in range(wide):
            for tile in range(2):
                if reach(x) + tile <= limit:
                    yield x, tile

    for x, tile in tiles(DEPTH - 1):
        here, other = enu[x, tile], enu[x, 1 - tile]
        east = 0.5 * (here + enu[(x + 1) % wide, tile])
        west = 0.5 * (here + enu[(x - 1) % wide, tile])
        north = 0.5 * (here + beside_y(here, other, True))
        south = 0.5 * (here + beside_y(here, other, False))
        ahead = jnp.where(lane == 127, 0.0, pltpu.roll(here, 127, 1))
        behind = jnp.where(lane == 0, 0.0, pltpu.roll(here, 1, 1))
        front = 0.5 * (here + ahead)
        back = 0.5 * (here + behind)
        coef[x, tile, 0] = 1.0 - (((east + west) + (north + south)) + (front + back))
        if x == size_x - 1:
            east = east * x_top
        if x == 0:
            west = west * x_low
        if tile == 0:
            north = jnp.where(sub == 7, north * y_top, north)
            south = jnp.where(sub == 0, south * y_low, south)
        coef[x, tile, 1], coef[x, tile, 2] = east, west
        coef[x, tile, 3], coef[x, tile, 4] = north, south
        coef[x, tile, 5] = jnp.where(lane == 127, 0.0, front)
        coef[x, tile, 6] = jnp.where(lane == 0, 0.0, back)

    for t in range(steps):
        src, dst = t % 2, (t + 1) % 2
        for x, tile in tiles(DEPTH - 1 - t):
            w = [coef[x, tile, i] for i in range(7)]
            for c in range(comps):
                here, other = ext[src, c, x, tile], ext[src, c, x, 1 - tile]
                new = w[0] * here
                new = new + w[1] * ext[src, c, (x + 1) % wide, tile]
                new = new + w[2] * ext[src, c, (x - 1) % wide, tile]
                new = new + w[3] * beside_y(here, other, True)
                new = new + w[4] * beside_y(here, other, False)
                new = new + w[5] * pltpu.roll(here, 127, 1)
                new = new + w[6] * pltpu.roll(here, 1, 1)
                push = ef[t, c, x, tile] if t < 3 else f[t, c, x]
                new = new + push
                if t < steps - 1:
                    ext[dst, c, x, tile] = new
                if tile == 0 and x < size_x:
                    snaps[t, c * size_x + x] = new
                    if t == steps - 1:
                        final[c, x] = new

    rows = kept.shape[0]
    slabs = kept.shape[1]
    n = rows + steps
    column = lax.broadcasted_iota(jnp.int32, (8, n), 1)
    total = square_a[...] + square_b[...]
    old = 0.5 * total[:, :n] + total[:, n:]
    scale = 1.0 / (slabs * 8 * 128 * nx * ny)
    for k0 in range(0, n, 8):
        acc = [[None] * 8 for _ in range(steps)]
        for s in range(slabs):
            new = [snaps[t, s] for t in range(steps)]
            for k in range(8):
                row = kept[k0 + k, s] if k0 + k < rows else new[k0 + k - rows]
                for t in range(steps):
                    if k0 + k >= rows and k0 + k - rows > t:
                        continue
                    term = row * new[t]
                    acc[t][k] = term if acc[t][k] is None else acc[t][k] + term
        block = old[k0 : k0 + 8]
        for t in range(steps):
            full = jnp.stack([jnp.zeros((8, 128), F32) if a is None else a for a in acc[t]], 0)
            summed = jnp.sum(pltpu.einshape("kyz->ykz", full), axis=0)
            entry = jnp.sum(summed, axis=1, keepdims=True)
            if k0 + 8 > rows:
                row_at = lax.broadcasted_iota(jnp.int32, (8, 1), 0) + k0
                entry = jnp.where(row_at == rows + t, 0.5 * entry, entry)
            block = jnp.where(column == rows + t, entry, block)
        part[pl.ds(k0, 8), :] = block * scale


def split(p):
    high = p.astype(BF16)
    return high, (p - high.astype(F32)).astype(BF16)


def to_rows(tiles):
    parts = [pltpu.einshape("kyz->ykz", tiles[k : k + 8]) for k in range(0, tiles.shape[0], 8)]
    return [jnp.concatenate([p[y] for p in parts], 0) for y in range(8)]


def from_rows(rows):
    n = rows[0].shape[0]
    return jnp.concatenate(
        [
            pltpu.einshape("ykz->kyz", jnp.stack([r[k : k + 8] for r in rows], 0))
            for k in range(0, n, 8)
        ],
        0,
    )


def square_of(kept, slabs, n, ready=None):
    rows = kept.shape[0]
    acc = None
    for s in slabs:
        if ready is not None:
            ready(s)
        tiles = jnp.concatenate([kept[:, s], jnp.zeros((n - rows, 8, 128), F32)], 0)
        lines = to_rows(tiles)
        for y in range(0, 8, 2):
            high, low = split(jnp.concatenate(lines[y : y + 2], 1))
            both = jnp.concatenate([high, low], 0)
            term = lax.dot_general(high, both, (((1,), (1,)), ((), ())), preferred_element_type=F32)
            acc = term if acc is None else acc + term
    return acc


def square_first_kernel(kept_in, kept, out, sems, *, n, count):
    slabs = kept.shape[1]
    step = slabs // sems.shape[0]
    copies = []
    for i in range(sems.shape[0]):
        at = (slice(None), pl.ds(i * step, step))
        copies.append(pltpu.make_async_copy(kept_in.at[at], kept.at[at], sems.at[i]))
    for copy in copies:
        copy.start()

    def ready(s):
        if s % step == 0:
            copies[s // step].wait()

    out[...] = square_of(kept, range(count), n, ready)
    for i in range(-(-count // step), len(copies)):
        copies[i].wait()


def square_rest_kernel(kept, out, *, n, count):
    out[...] = square_of(kept, range(count, kept.shape[1]), n)


def factor_of(gram):
    n = gram.shape[0]
    count = n // 8
    sub = sub_index()
    row_at = lax.broadcasted_iota(jnp.int32, (n, n), 0)
    col_at = lax.broadcasted_iota(jnp.int32, (n, n), 1)
    eye = jnp.where(row_at == col_at, 1.0, 0.0).astype(F32)
    whole = jnp.concatenate([gram, eye], 1)
    w = [whole[8 * c : 8 * c + 8] for c in range(count)]

    def spread(tile, j):
        return jnp.broadcast_to(tile[:, j : j + 1], tile.shape)

    def pick(tile, q):
        return jnp.broadcast_to(tile[q : q + 1, :], tile.shape)

    for b in range(count):
        cols = {c: [spread(w[c], 8 * b + q) for q in range(8)] for c in range(b, count)}
        pivots = jnp.ones(w[b].shape, F32)
        for q in range(8):
            head = [pick(cols[b][r], q) for r in range(q, 8)]
            inverse = 1.0 / head[0]
            pivots = jnp.where(sub == q, head[0], pivots)
            line = pick(w[b], q)
            for c in range(b, count):
                ratio = cols[c][q] * inverse
                if c == b:
                    ratio = jnp.where(sub > q, ratio, 0.0)
                w[c] = w[c] - ratio * line
                for r in range(q + 1, 8):
                    cols[c][r] = cols[c][r] - ratio * head[r - q]
        w[b] = w[b] * lax.rsqrt(pivots)
    return jnp.concatenate(w, 0)


def halves_kernel(kept, snaps, panel):
    n = panel.shape[1] // 2
    for s in range(kept.shape[1]):
        lines = to_rows(jnp.concatenate([kept[:, s], snaps[:, s]], 0))
        for i in range(4):
            high, low = split(jnp.concatenate(lines[2 * i : 2 * i + 2], 1))
            panel[4 * s + i, :n], panel[4 * s + i, n:] = high, low


def basis_kernel(part, panel, basis, factor, out, sems):
    n = part.shape[0]
    slabs = panel.shape[0] // 4
    block = slabs // sems.shape[0]
    m = part[...]
    w = factor_of(m + m.T)
    row_at = lax.broadcasted_iota(jnp.int32, (n, n), 0)
    col_at = lax.broadcasted_iota(jnp.int32, (n, n), 1)
    factor[...] = jnp.where(row_at <= col_at, w[:, :n], 0.0)
    high, low = split(w[:, n:])
    lhs = jnp.concatenate([high, high, low], 1)
    copies = []
    for s in range(slabs):
        pieces = []
        for i in range(4):
            both = panel[4 * s + i]
            rhs = jnp.concatenate([both, both[:n]], 0)
            r = lax.dot_general(lhs, rhs, (((1,), (0,)), ((), ())), preferred_element_type=F32)
            pieces += [r[:, :128], r[:, 128:]]
        out[:, s] = from_rows(pieces)
        if (s + 1) % block == 0:
            at = (slice(None), pl.ds(s + 1 - block, block))
            copy = pltpu.make_async_copy(out.at[at], basis.at[at], sems.at[s // block])
            copy.start()
            copies.append(copy)
    for copy in copies:
        copy.wait()


def pair_exchange(first, second, axis):
    count = lax.axis_size(axis)
    near = [(i, i ^ 1) for i in range(count)]
    far = [(i, ((i + 1) ^ 1) - 1) for i in range(1, count - 1)]
    distant = lax.ppermute(second, axis, far)
    return lax.ppermute(first, axis, near), distant


def sum_over(value, minor, major):
    inner, outer = lax.axis_size(minor), lax.axis_size(major)
    count = inner * outer
    if count & (count - 1):
        return lax.psum(value, (major, minor))
    low = [1 << i for i in range(inner.bit_length() - 1)]
    high = [inner << i for i in range(outer.bit_length() - 1)]
    both = min(len(low), len(high))
    groups = [[high[i], low[i]] for i in range(both)]
    rest = low[both:] + high[both:]
    groups += [rest[i : i + 2] for i in range(0, len(rest), 2)]
    for group in groups:
        masks = group + ([group[0] ^ group[1]] if len(group) == 2 else [])
        others = [
            lax.ppermute(value, (major, minor), [(i, i ^ m) for i in range(count)]) for m in masks
        ]
        for other in others:
            value = value + other
    return value


def local(velocity, viscosity, forcing, earlier):
    comps, size_x = velocity.shape[0], velocity.shape[1]
    steps, rows = forcing.shape[0], earlier.shape[0]
    n, slabs = rows + steps, comps * size_x
    half = (2 * slabs + size_x + slabs // 2) // 2
    call = pl.pallas_call
    v, nu, f, send_a, send_b = call(
        pack_y_kernel,
        out_shape=(
            struct(*velocity.shape),
            struct(*viscosity.shape),
            struct(*forcing.shape),
            struct(half, 8, 128),
            struct(half, 8, 128),
        ),
        in_specs=[HBM] * 3,
        out_specs=(VMEM,) * 5,
        scratch_shapes=[pltpu.SemaphoreType.DMA((3,))],
        compiler_params=limit(8),
        name="pack_y",
    )(*[pltpu.with_memory_space_constraint(a, pltpu.HBM) for a in (velocity, viscosity, forcing)])
    recv_a, recv_b = pair_exchange(send_a, send_b, "gy")
    first = slabs * 2 // 3
    kept, square_a = call(
        functools.partial(square_first_kernel, n=n, count=first),
        out_shape=(struct(rows, slabs, 8, 128), struct(n, 2 * n)),
        in_specs=[HBM],
        out_specs=(VMEM,) * 2,
        scratch_shapes=[pltpu.SemaphoreType.DMA((6,))],
        compiler_params=limit(8),
        name="gram_first",
    )(pltpu.with_memory_space_constraint(earlier.reshape(rows, slabs, 8, 128), pltpu.HBM))
    own, rim = x_items(comps)
    wire = struct(len(own) + len(rim), 8, 128)
    rv, rnu, rf, send_a, send_b = call(
        pack_x_kernel,
        out_shape=(
            struct(*velocity.shape),
            struct(*viscosity.shape),
            struct(3, *velocity.shape),
            wire,
            wire,
        ),
        in_specs=[VMEM] * 5 + [pl.BlockSpec(memory_space=pl.ANY)],
        out_specs=(VMEM,) * 5,
        compiler_params=limit(8),
        name="pack_x",
    )(v, nu, f, recv_a, recv_b, square_a)
    recv_a, recv_b = pair_exchange(send_a, send_b, "gx")
    square_b = call(
        functools.partial(square_rest_kernel, n=n, count=first),
        out_shape=struct(n, 2 * n),
        in_specs=[VMEM],
        out_specs=VMEM,
        compiler_params=limit(8),
        name="gram_rest",
    )(kept)
    snaps, final, part = call(
        steps_kernel,
        out_shape=(struct(steps, slabs, 8, 128), struct(*velocity.shape), struct(n, n)),
        in_specs=[VMEM] * 11,
        out_specs=(VMEM,) * 3,
        scratch_shapes=[
            pltpu.VMEM((2, comps, 2 * size_x, 2, 8, 128), F32),
            pltpu.VMEM((2 * size_x, 2, 8, 128), F32),
            pltpu.VMEM((3, comps, 2 * size_x, 2, 8, 128), F32),
            pltpu.VMEM((2 * size_x, 2, 7, 8, 128), F32),
        ],
        compiler_params=limit(12),
        name="steps",
    )(v, nu, f, rv, rnu, rf, recv_a, recv_b, kept, square_a, square_b)
    panel = call(
        halves_kernel,
        out_shape=jax.ShapeDtypeStruct((4 * slabs, 2 * n, 256), BF16),
        in_specs=[VMEM] * 2,
        out_specs=VMEM,
        compiler_params=limit(8),
        name="halves",
    )(kept, snaps)
    part = sum_over(part, "gy", "gx")
    basis, factor = call(
        basis_kernel,
        out_shape=(struct(n, slabs, 8, 128), struct(n, n)),
        in_specs=[VMEM] * 2,
        out_specs=(HBM, VMEM),
        scratch_shapes=[pltpu.VMEM((n, slabs, 8, 128), F32), pltpu.SemaphoreType.DMA((slabs // 3,))],
        compiler_params=limit(16),
        name="factor_basis",
    )(part, panel)
    return final, basis.reshape((n,) + velocity.shape), factor


def solution(mesh):
    return jax.shard_map(
        local,
        mesh=mesh,
        in_specs=(
            P(None, "gx", "gy", None),
            P("gx", "gy", None),
            P(None, None, "gx", "gy", None),
            P(None, None, "gx", "gy", None),
        ),
        out_specs=(P(None, "gx", "gy", None), P(None, None, "gx", "gy", None), P()),
        check_vma=False,
    )
```

```python
import functools
import jax
import jax.numpy as jnp
from jax import lax
from jax.experimental import pallas as pl
from jax.experimental.pallas import tpu as pltpu
from jax.sharding import PartitionSpec as P

F32 = jnp.float32
BF16 = jnp.bfloat16
DEPTH = 4
VMEM = pl.BlockSpec(memory_space=pltpu.VMEM)
HBM = pl.BlockSpec(memory_space=pltpu.HBM)


def limit(mib):
    return pltpu.CompilerParams(vmem_limit_bytes=mib << 20)


def struct(*shape):
    return jax.ShapeDtypeStruct(shape, F32)


def sub_index():
    return lax.broadcasted_iota(jnp.int32, (8, 128), 0)


def turn(tile, shift):
    return pltpu.roll(tile, shift, 0)


def y_items(v, nu, f, up):
    sub = sub_index()
    comps, size_x = v.shape[0], v.shape[1]
    cells = [(c, x) for c in range(comps) for x in range(size_x)]
    items = [v[c, x] for c, x in cells] + [nu[x] for x in range(size_x)]
    for c, x in cells:
        if up:
            items.append(jnp.where(sub == 4, turn(f[2, c, x], 5), f[0, c, x]))
        else:
            items.append(jnp.where(sub == 3, turn(f[2, c, x], 3), f[0, c, x]))
    for (c, x), (d, w) in zip(cells[0::2], cells[1::2]):
        if up:
            items.append(jnp.where(sub >= 6, f[1, c, x], turn(f[1, d, w], 6)))
        else:
            items.append(jnp.where(sub < 2, f[1, c, x], turn(f[1, d, w], 2)))
    return items


def pack_y_kernel(v_in, nu_in, f_in, v, nu, f, send_a, send_b, sems):
    pairs = ((f_in, f), (v_in, v), (nu_in, nu))
    copies = [pltpu.make_async_copy(a, b, sems.at[i]) for i, (a, b) in enumerate(pairs)]
    for copy in copies:
        copy.start()
    for copy in copies:
        copy.wait()
    sub = sub_index()
    even = lax.rem(lax.axis_index("gy"), 2) == 0
    upper, lower = (y_items(v, nu, f, True), y_items(v, nu, f, False))
    half = send_a.shape[0]
    for j in range(half):
        to_up = jnp.where(sub >= 4, upper[j], turn(upper[half + j], 4))
        to_down = jnp.where(sub < 4, lower[j], turn(lower[half + j], 4))
        send_a[j] = jnp.where(even, to_up, to_down)
        send_b[j] = jnp.where(even, to_down, to_up)


def unpack_y(recv_a, recv_b, even, j):
    sub = sub_index()
    half = recv_a.shape[0]
    k = j % half
    a, b = recv_a[k], recv_b[k]
    above, below = jnp.where(even, a, b), jnp.where(even, b, a)
    if j < half:
        return jnp.where(sub < 4, above, below)
    return turn(jnp.where(sub < 4, below, above), 4)


def x_items(comps):
    own = [("v", c, d) for c in range(comps) for d in range(1, 5)]
    own += [("nu", 0, d) for d in range(1, 5)]
    for t in range(3):
        own += [(t, c, d) for c in range(comps) for d in range(1, 4 - t)]
    rim = [("v", c, d) for c in range(comps) for d in range(1, 4)]
    rim += [("nu", 0, d) for d in range(1, 4)]
    for t in range(2):
        rim += [(t, c, d) for c in range(comps) for d in range(1, 3 - t)]
    return own, rim


def pack_x_kernel(v, nu, f, recv_a, recv_b, after, rv, rnu, rf, send_a, send_b):
    sub = sub_index()
    even_y = lax.rem(lax.axis_index("gy"), 2) == 0
    even_x = lax.rem(lax.axis_index("gx"), 2) == 0
    comps, size_x = v.shape[0], v.shape[1]
    cells = [(c, x) for c in range(comps) for x in range(size_x)]
    get = functools.partial(unpack_y, recv_a, recv_b, even_y)
    at = 0
    for c, x in cells:
        rv[c, x] = get(at)
        at += 1
    for x in range(size_x):
        rnu[x] = get(at)
        at += 1
    for c, x in cells:
        item = get(at)
        rf[0, c, x] = item
        rf[2, c, x] = jnp.where(sub < 4, turn(item, 5), turn(item, 3))
        at += 1
    for (c, x), (d, w) in zip(cells[0::2], cells[1::2]):
        item = get(at)
        rf[1, c, x] = item
        rf[1, d, w] = jnp.where(sub < 4, turn(item, 6), turn(item, 2))
        at += 1
    own, rim = x_items(comps)
    at = 0
    for group, (gv, gnu, gf) in ((own, (v, nu, f)), (rim, (rv, rnu, rf))):
        for name, c, d in group:
            high, low = size_x - d, d - 1
            for ref, x in (
                (send_a, jnp.where(even_x, high, low)),
                (send_b, jnp.where(even_x, low, high)),
            ):
                if name == "v":
                    ref[at] = gv[c, x]
                elif name == "nu":
                    ref[at] = gnu[x]
                else:
                    ref[at] = gf[name, c, x]
            at += 1


def beside_y(first, second, up):
    sub = sub_index()
    if up:
        return jnp.where(sub == 7, turn(second, 7), turn(first, 7))
    return jnp.where(sub == 0, turn(second, 1), turn(first, 1))


def steps_kernel(v, nu, f, rv, rnu, rf, recv_a, recv_b, kept, square_a, square_b, snaps, final, part, ext, enu, ef, coef, sem):
    comps, size_x = v.shape[0], v.shape[1]
    steps = f.shape[0]
    wide = 2 * size_x
    ix, nx = lax.axis_index("gx"), lax.axis_size("gx")
    iy, ny = lax.axis_index("gy"), lax.axis_size("gy")
    even = lax.rem(ix, 2) == 0
    sub = sub_index()
    lane = lax.broadcasted_iota(jnp.int32, (8, 128), 1)
    one = lambda flag: jnp.where(flag, 1.0, 0.0).astype(F32)
    x_top, x_low = one(ix < nx - 1), one(ix > 0)
    y_top, y_low = one(iy < ny - 1), one(iy > 0)

    for x in range(size_x):
        enu[x, 0], enu[x, 1] = nu[x], rnu[x]
        for c in range(comps):
            ext[0, c, x, 0], ext[0, c, x, 1] = v[c, x], rv[c, x]
            for t in range(3):
                ef[t, c, x, 0], ef[t, c, x, 1] = f[t, c, x], rf[t, c, x]
    own, rim = x_items(comps)
    at = 0
    for tile, group in enumerate((own, rim)):
        for name, c, d in group:
            high, low = size_x - 1 + d, wide - d
            for ref, x in (
                (recv_a, jnp.where(even, high, low)),
                (recv_b, jnp.where(even, low, high)),
            ):
                if name == "v":
                    ext[0, c, x, tile] = ref[at]
                elif name == "nu":
                    enu[x, tile] = ref[at]
                else:
                    ef[name, c, x, tile] = ref[at]
            at += 1

    def reach(x):
        return 0 if x < size_x else min(x - size_x + 1, wide - x)

    def tiles(limit):
        for x in range(wide):
            for tile in range(2):
                if reach(x) + tile <= limit:
                    yield x, tile

    for x, tile in tiles(DEPTH - 1):
        here, other = enu[x, tile], enu[x, 1 - tile]
        east = 0.5 * (here + enu[(x + 1) % wide, tile])
        west = 0.5 * (here + enu[(x - 1) % wide, tile])
        north = 0.5 * (here + beside_y(here, other, True))
        south = 0.5 * (here + beside_y(here, other, False))
        ahead = jnp.where(lane == 127, 0.0, pltpu.roll(here, 127, 1))
        behind = jnp.where(lane == 0, 0.0, pltpu.roll(here, 1, 1))
        front = 0.5 * (here + ahead)
        back = 0.5 * (here + behind)
        coef[x, tile, 0] = 1.0 - (((east + west) + (north + south)) + (front + back))
        if x == size_x - 1:
            east = east * x_top
        if x == 0:
            west = west * x_low
        if tile == 0:
            north = jnp.where(sub == 7, north * y_top, north)
            south = jnp.where(sub == 0, south * y_low, south)
        coef[x, tile, 1], coef[x, tile, 2] = east, west
        coef[x, tile, 3], coef[x, tile, 4] = north, south
        coef[x, tile, 5] = jnp.where(lane == 127, 0.0, front)
        coef[x, tile, 6] = jnp.where(lane == 0, 0.0, back)

    for t in range(steps):
        src, dst = t % 2, (t + 1) % 2
        for x, tile in tiles(DEPTH - 1 - t):
            w = [coef[x, tile, i] for i in range(7)]
            for c in range(comps):
                here, other = ext[src, c, x, tile], ext[src, c, x, 1 - tile]
                new = w[0] * here
                new = new + w[1] * ext[src, c, (x + 1) % wide, tile]
                new = new + w[2] * ext[src, c, (x - 1) % wide, tile]
                new = new + w[3] * beside_y(here, other, True)
                new = new + w[4] * beside_y(here, other, False)
                new = new + w[5] * pltpu.roll(here, 127, 1)
                new = new + w[6] * pltpu.roll(here, 1, 1)
                push = ef[t, c, x, tile] if t < 3 else f[t, c, x]
                new = new + push
                if t < steps - 1:
                    ext[dst, c, x, tile] = new
                if tile == 0 and x < size_x:
                    snaps[t, c * size_x + x] = new

    last = pltpu.make_async_copy(snaps.at[steps - 1], final, sem.at[0])
    last.start()

    rows = kept.shape[0]
    slabs = kept.shape[1]
    n = rows + steps
    column = lax.broadcasted_iota(jnp.int32, (8, n), 1)
    total = square_a[...] + square_b[...]
    old = 0.5 * total[:, :n] + total[:, n:]
    scale = 1.0 / (slabs * 8 * 128 * nx * ny)
    for k0 in range(0, n, 8):
        acc = [[None] * 8 for _ in range(steps)]
        for s in range(slabs):
            new = [snaps[t, s] for t in range(steps)]
            for k in range(8):
                row = kept[k0 + k, s] if k0 + k < rows else new[k0 + k - rows]
                for t in range(steps):
                    if k0 + k >= rows and k0 + k - rows > t:
                        continue
                    term = row * new[t]
                    acc[t][k] = term if acc[t][k] is None else acc[t][k] + term
        block = old[k0 : k0 + 8]
        for t in range(steps):
            full = jnp.stack([jnp.zeros((8, 128), F32) if a is None else a for a in acc[t]], 0)
            summed = jnp.sum(pltpu.einshape("kyz->ykz", full), axis=0)
            entry = jnp.sum(summed, axis=1, keepdims=True)
            if k0 + 8 > rows:
                row_at = lax.broadcasted_iota(jnp.int32, (8, 1), 0) + k0
                entry = jnp.where(row_at == rows + t, 0.5 * entry, entry)
            block = jnp.where(column == rows + t, entry, block)
        part[pl.ds(k0, 8), :] = block * scale
    last.wait()


def split(p):
    high = p.astype(BF16)
    return high, (p - high.astype(F32)).astype(BF16)


def to_rows(tiles):
    parts = [pltpu.einshape("kyz->ykz", tiles[k : k + 8]) for k in range(0, tiles.shape[0], 8)]
    return [jnp.concatenate([p[y] for p in parts], 0) for y in range(8)]


def from_rows(rows):
    n = rows[0].shape[0]
    return jnp.concatenate(
        [
            pltpu.einshape("ykz->kyz", jnp.stack([r[k : k + 8] for r in rows], 0))
            for k in range(0, n, 8)
        ],
        0,
    )


def square_of(kept, slabs, n, ready=None):
    rows = kept.shape[0]
    acc = None
    for s in slabs:
        if ready is not None:
            ready(s)
        tiles = jnp.concatenate([kept[:, s], jnp.zeros((n - rows, 8, 128), F32)], 0)
        lines = to_rows(tiles)
        for y in range(0, 8, 2):
            high, low = split(jnp.concatenate(lines[y : y + 2], 1))
            both = jnp.concatenate([high, low], 0)
            term = lax.dot_general(high, both, (((1,), (1,)), ((), ())), preferred_element_type=F32)
            acc = term if acc is None else acc + term
    return acc


def square_first_kernel(kept_in, kept, out, sems, *, n, count):
    slabs = kept.shape[1]
    step = slabs // sems.shape[0]
    copies = []
    for i in range(sems.shape[0]):
        at = (slice(None), pl.ds(i * step, step))
        copies.append(pltpu.make_async_copy(kept_in.at[at], kept.at[at], sems.at[i]))
    ahead = 3
    for copy in copies[:ahead]:
        copy.start()

    def arrive(i):
        copies[i].wait()
        if i + ahead < len(copies):
            copies[i + ahead].start()

    def ready(s):
        if s % step == 0:
            arrive(s // step)

    out[...] = square_of(kept, range(count), n, ready)
    for i in range(-(-count // step), len(copies)):
        arrive(i)


def square_rest_kernel(kept, out, *, n, count):
    out[...] = square_of(kept, range(count, kept.shape[1]), n)


def eliminate(w, b):
    sub = sub_index()
    count = len(w)

    def spread(tile, j):
        return jnp.broadcast_to(tile[:, j : j + 1], tile.shape)

    def pick(tile, q):
        return jnp.broadcast_to(tile[q : q + 1, :], tile.shape)

    cols = {c: [spread(w[c], 8 * b + q) for q in range(8)] for c in range(b, count)}
    pivots = jnp.ones(w[b].shape, F32)
    for q in range(8):
        head = [pick(cols[b][r], q) for r in range(q, 8)]
        inverse = 1.0 / head[0]
        pivots = jnp.where(sub == q, head[0], pivots)
        line = pick(w[b], q)
        for c in range(b, count):
            ratio = cols[c][q] * inverse
            if c == b:
                ratio = jnp.where(sub > q, ratio, 0.0)
            w[c] = w[c] - ratio * line
            for r in range(q + 1, 8):
                cols[c][r] = cols[c][r] - ratio * head[r - q]
    w[b] = w[b] * lax.rsqrt(pivots)


def halves_kernel(kept, snaps, panel):
    n = panel.shape[1] // 2
    for s in range(kept.shape[1]):
        lines = to_rows(jnp.concatenate([kept[:, s], snaps[:, s]], 0))
        for i in range(4):
            high, low = split(jnp.concatenate(lines[2 * i : 2 * i + 2], 1))
            panel[4 * s + i, :n], panel[4 * s + i, n:] = high, low


def basis_kernel(part, panel, basis, factor, out, upper, sems, sem):
    n = part.shape[0]
    mid = n // 2
    slabs = panel.shape[0] // 4
    batches = sems.shape[1]
    block = slabs // batches
    m = part[...]
    row_at = lax.broadcasted_iota(jnp.int32, (n, n), 0)
    col_at = lax.broadcasted_iota(jnp.int32, (n, n), 1)
    eye = jnp.where(row_at == col_at, 1.0, 0.0).astype(F32)
    whole = jnp.concatenate([m + m.T, eye], 1)
    w = [whole[c : c + 8] for c in range(0, n, 8)]
    copies = []

    def rows_of(first, last, between):
        inverse = jnp.concatenate(w[first // 8 : last // 8], 0)[:, n : n + last]
        high, low = split(inverse)
        top = jnp.concatenate([high, high], 1)
        lhs = jnp.concatenate([top, jnp.concatenate([low, jnp.zeros_like(low)], 1)], 0)
        for s in range(slabs):
            pieces = []
            for i in range(4):
                high, low = panel[4 * s + i, :last], panel[4 * s + i, n : n + last]
                rhs = jnp.concatenate([high, low], 0)
                r = lax.dot_general(lhs, rhs, (((1,), (0,)), ((), ())), preferred_element_type=F32)
                r = r[: last - first] + r[last - first :]
                pieces += [r[:, :128], r[:, 128:]]
            out[first:last, s] = from_rows(pieces)
            between(s)
            if (s + 1) % block == 0:
                at = (pl.ds(first, last - first), pl.ds(s + 1 - block, block))
                sem = sems.at[0 if first == 0 else 1, s // block]
                copy = pltpu.make_async_copy(out.at[at], basis.at[at], sem)
                copy.start()
                copies.append(copy)

    half = mid // 8
    for b in range(half):
        eliminate(w, b)
    pace = slabs // half

    def go_on(s):
        if (s + 1) % pace == 0 and (s + 1) // pace <= half:
            eliminate(w, half + (s + 1) // pace - 1)

    rows_of(0, mid, go_on)
    upper[...] = jnp.where(row_at <= col_at, jnp.concatenate(w, 0)[:, :n], 0.0)
    copies.append(pltpu.make_async_copy(upper, factor, sem.at[0]))
    copies[-1].start()
    rows_of(mid, n, lambda s: None)
    for copy in copies:
        copy.wait()


def pair_exchange(first, second, axis):
    count = lax.axis_size(axis)
    near = [(i, i ^ 1) for i in range(count)]
    far = [(i, ((i + 1) ^ 1) - 1) for i in range(1, count - 1)]
    distant = lax.ppermute(second, axis, far)
    return lax.ppermute(first, axis, near), distant


def sum_over(value, minor, major):
    inner, outer = lax.axis_size(minor), lax.axis_size(major)
    count = inner * outer
    if count & (count - 1):
        return lax.psum(value, (major, minor))
    low = [1 << i for i in range(inner.bit_length() - 1)]
    high = [inner << i for i in range(outer.bit_length() - 1)]
    both = min(len(low), len(high))
    groups = [[high[i], low[i]] for i in range(both)]
    rest = low[both:] + high[both:]
    groups += [rest[i : i + 2] for i in range(0, len(rest), 2)]
    for group in groups:
        masks = group + ([group[0] ^ group[1]] if len(group) == 2 else [])
        others = [
            lax.ppermute(value, (major, minor), [(i, i ^ m) for i in range(count)]) for m in masks
        ]
        for other in others:
            value = value + other
    return value


def local(velocity, viscosity, forcing, earlier):
    comps, size_x = velocity.shape[0], velocity.shape[1]
    steps, rows = forcing.shape[0], earlier.shape[0]
    n, slabs = rows + steps, comps * size_x
    half = (2 * slabs + size_x + slabs // 2) // 2
    call = pl.pallas_call
    v, nu, f, send_a, send_b = call(
        pack_y_kernel,
        out_shape=(
            struct(*velocity.shape),
            struct(*viscosity.shape),
            struct(*forcing.shape),
            struct(half, 8, 128),
            struct(half, 8, 128),
        ),
        in_specs=[HBM] * 3,
        out_specs=(VMEM,) * 5,
        scratch_shapes=[pltpu.SemaphoreType.DMA((3,))],
        compiler_params=limit(8),
        name="pack_y",
    )(*[pltpu.with_memory_space_constraint(a, pltpu.HBM) for a in (velocity, viscosity, forcing)])
    recv_a, recv_b = pair_exchange(send_a, send_b, "gy")
    first = slabs * 2 // 3
    kept, square_a = call(
        functools.partial(square_first_kernel, n=n, count=first),
        out_shape=(struct(rows, slabs, 8, 128), struct(n, 2 * n)),
        in_specs=[HBM],
        out_specs=(VMEM,) * 2,
        scratch_shapes=[pltpu.SemaphoreType.DMA((6,))],
        compiler_params=limit(8),
        name="gram_first",
    )(pltpu.with_memory_space_constraint(earlier.reshape(rows, slabs, 8, 128), pltpu.HBM))
    own, rim = x_items(comps)
    wire = struct(len(own) + len(rim), 8, 128)
    rv, rnu, rf, send_a, send_b = call(
        pack_x_kernel,
        out_shape=(
            struct(*velocity.shape),
            struct(*viscosity.shape),
            struct(3, *velocity.shape),
            wire,
            wire,
        ),
        in_specs=[VMEM] * 5 + [pl.BlockSpec(memory_space=pl.ANY)],
        out_specs=(VMEM,) * 5,
        compiler_params=limit(8),
        name="pack_x",
    )(v, nu, f, recv_a, recv_b, square_a)
    recv_a, recv_b = pair_exchange(send_a, send_b, "gx")
    square_b = call(
        functools.partial(square_rest_kernel, n=n, count=first),
        out_shape=struct(n, 2 * n),
        in_specs=[VMEM],
        out_specs=VMEM,
        compiler_params=limit(8),
        name="gram_rest",
    )(kept)
    snaps, final, part = call(
        steps_kernel,
        out_shape=(struct(steps, slabs, 8, 128), struct(slabs, 8, 128), struct(n, n)),
        in_specs=[VMEM] * 11,
        out_specs=(VMEM, HBM, VMEM),
        scratch_shapes=[
            pltpu.VMEM((2, comps, 2 * size_x, 2, 8, 128), F32),
            pltpu.VMEM((2 * size_x, 2, 8, 128), F32),
            pltpu.VMEM((3, comps, 2 * size_x, 2, 8, 128), F32),
            pltpu.VMEM((2 * size_x, 2, 7, 8, 128), F32),
            pltpu.SemaphoreType.DMA((1,)),
        ],
        compiler_params=limit(12),
        name="steps",
    )(v, nu, f, rv, rnu, rf, recv_a, recv_b, kept, square_a, square_b)
    panel = call(
        halves_kernel,
        out_shape=jax.ShapeDtypeStruct((4 * slabs, 2 * n, 256), BF16),
        in_specs=[VMEM] * 2,
        out_specs=VMEM,
        compiler_params=limit(8),
        name="halves",
    )(kept, snaps)
    part = sum_over(part, "gy", "gx")
    basis, factor = call(
        basis_kernel,
        out_shape=(struct(n, slabs, 8, 128), struct(n, n)),
        in_specs=[VMEM] * 2,
        out_specs=(HBM, HBM),
        scratch_shapes=[
            pltpu.VMEM((n, slabs, 8, 128), F32),
            pltpu.VMEM((n, n), F32),
            pltpu.SemaphoreType.DMA((2, slabs // 3)),
            pltpu.SemaphoreType.DMA((1,)),
        ],
        compiler_params=limit(16),
        name="factor_basis",
    )(part, panel)
    return final.reshape(velocity.shape), basis.reshape((n,) + velocity.shape), factor


def solution(mesh):
    return jax.shard_map(
        local,
        mesh=mesh,
        in_specs=(
            P(None, "gx", "gy", None),
            P("gx", "gy", None),
            P(None, None, "gx", "gy", None),
            P(None, None, "gx", "gy", None),
        ),
        out_specs=(P(None, "gx", "gy", None), P(None, None, "gx", "gy", None), P()),
        check_vma=False,
    )
```

```python
import functools
import jax
import jax.numpy as jnp
from jax import lax
from jax.experimental import pallas as pl
from jax.experimental.pallas import tpu as pltpu
from jax.sharding import PartitionSpec as P

F32 = jnp.float32
BF16 = jnp.bfloat16
DEPTH = 4
VMEM = pl.BlockSpec(memory_space=pltpu.VMEM)
HBM = pl.BlockSpec(memory_space=pltpu.HBM)


def limit(mib):
    return pltpu.CompilerParams(vmem_limit_bytes=mib << 20)


def struct(*shape):
    return jax.ShapeDtypeStruct(shape, F32)


def sub_index():
    return lax.broadcasted_iota(jnp.int32, (8, 128), 0)


def turn(tile, shift):
    return pltpu.roll(tile, shift, 0)


def y_items(v, nu, f, up):
    sub = sub_index()
    comps, size_x = v.shape[0], v.shape[1]
    cells = [(c, x) for c in range(comps) for x in range(size_x)]
    items = [v[c, x] for c, x in cells] + [nu[x] for x in range(size_x)]
    for c, x in cells:
        if up:
            items.append(jnp.where(sub == 4, turn(f[2, c, x], 5), f[0, c, x]))
        else:
            items.append(jnp.where(sub == 3, turn(f[2, c, x], 3), f[0, c, x]))
    for (c, x), (d, w) in zip(cells[0::2], cells[1::2]):
        if up:
            items.append(jnp.where(sub >= 6, f[1, c, x], turn(f[1, d, w], 6)))
        else:
            items.append(jnp.where(sub < 2, f[1, c, x], turn(f[1, d, w], 2)))
    return items


def pack_y_kernel(v_in, nu_in, f_in, v, nu, f, send_a, send_b, sems):
    pairs = ((f_in, f), (v_in, v), (nu_in, nu))
    copies = [pltpu.make_async_copy(a, b, sems.at[i]) for i, (a, b) in enumerate(pairs)]
    for copy in copies:
        copy.start()
    for copy in copies:
        copy.wait()
    sub = sub_index()
    even = lax.rem(lax.axis_index("gy"), 2) == 0
    upper, lower = (y_items(v, nu, f, True), y_items(v, nu, f, False))
    half = send_a.shape[0]
    for j in range(half):
        to_up = jnp.where(sub >= 4, upper[j], turn(upper[half + j], 4))
        to_down = jnp.where(sub < 4, lower[j], turn(lower[half + j], 4))
        send_a[j] = jnp.where(even, to_up, to_down)
        send_b[j] = jnp.where(even, to_down, to_up)


def unpack_y(recv_a, recv_b, even, j):
    sub = sub_index()
    half = recv_a.shape[0]
    k = j % half
    a, b = recv_a[k], recv_b[k]
    above, below = jnp.where(even, a, b), jnp.where(even, b, a)
    if j < half:
        return jnp.where(sub < 4, above, below)
    return turn(jnp.where(sub < 4, below, above), 4)


def x_items(comps):
    own = [("v", c, d) for c in range(comps) for d in range(1, 5)]
    own += [("nu", 0, d) for d in range(1, 5)]
    for t in range(3):
        own += [(t, c, d) for c in range(comps) for d in range(1, 4 - t)]
    fields = [("v", c) for c in range(comps)] + [("nu", 0)]
    rim = [((name, c, 1), (name, c, 3), 3) for name, c in fields]
    four = [(name, c, 2) for name, c in fields] + [(0, c, 1) for c in range(comps)]
    four += [(0, c, 2) for c in range(comps)] + [(1, c, 1) for c in range(comps)]
    rim += [(one, two, 2) for one, two in zip(four[0::2], four[1::2])]
    rim += [(one, None, 0) for one in four[len(four) - len(four) % 2 :]]
    return own, rim


def merge(first, second, shift):
    sub = sub_index()
    if shift == 3:
        above, below = sub == 3, sub == 4
    else:
        above, below = (sub >= 2) & (sub < 4), (sub >= 4) & (sub < 6)
    return jnp.where(above, turn(second, shift), jnp.where(below, turn(second, 8 - shift), first))


def unmerge(tile, shift):
    return jnp.where(sub_index() < 4, turn(tile, 8 - shift), turn(tile, shift))


def pack_x_kernel(v, nu, f, recv_a, recv_b, after, rv, rnu, rf, send_a, send_b):
    sub = sub_index()
    even_y = lax.rem(lax.axis_index("gy"), 2) == 0
    even_x = lax.rem(lax.axis_index("gx"), 2) == 0
    comps, size_x = v.shape[0], v.shape[1]
    cells = [(c, x) for c in range(comps) for x in range(size_x)]
    get = functools.partial(unpack_y, recv_a, recv_b, even_y)
    at = 0
    for c, x in cells:
        rv[c, x] = get(at)
        at += 1
    for x in range(size_x):
        rnu[x] = get(at)
        at += 1
    for c, x in cells:
        item = get(at)
        rf[0, c, x] = item
        rf[2, c, x] = jnp.where(sub < 4, turn(item, 5), turn(item, 3))
        at += 1
    for (c, x), (d, w) in zip(cells[0::2], cells[1::2]):
        item = get(at)
        rf[1, c, x] = item
        rf[1, d, w] = jnp.where(sub < 4, turn(item, 6), turn(item, 2))
        at += 1
    own, rim = x_items(comps)

    def take(source, item, upward):
        name, c, d = item
        field, viscosity, push = source
        x = jnp.where(upward, size_x - d, d - 1)
        if name == "v":
            return field[c, x]
        return viscosity[x] if name == "nu" else push[name, c, x]

    for send, upward in ((send_a, even_x), (send_b, jnp.logical_not(even_x))):
        for at, item in enumerate(own):
            send[at] = take((v, nu, f), item, upward)
        for at, (one, two, shift) in enumerate(rim):
            tile = take((rv, rnu, rf), one, upward)
            if two is not None:
                tile = merge(tile, take((rv, rnu, rf), two, upward), shift)
            send[len(own) + at] = tile


def beside_y(first, second, up):
    sub = sub_index()
    if up:
        return jnp.where(sub == 7, turn(second, 7), turn(first, 7))
    return jnp.where(sub == 0, turn(second, 1), turn(first, 1))


def steps_kernel(v, nu, f, rv, rnu, rf, recv_a, recv_b, kept, square_a, square_b, snaps, final, part, ext, enu, ef, coef, sem):
    comps, size_x = v.shape[0], v.shape[1]
    steps = f.shape[0]
    wide = 2 * size_x
    ix, nx = lax.axis_index("gx"), lax.axis_size("gx")
    iy, ny = lax.axis_index("gy"), lax.axis_size("gy")
    even = lax.rem(ix, 2) == 0
    sub = sub_index()
    lane = lax.broadcasted_iota(jnp.int32, (8, 128), 1)
    one = lambda flag: jnp.where(flag, 1.0, 0.0).astype(F32)
    x_top, x_low = one(ix < nx - 1), one(ix > 0)
    y_top, y_low = one(iy < ny - 1), one(iy > 0)

    for x in range(size_x):
        enu[x, 0], enu[x, 1] = nu[x], rnu[x]
        for c in range(comps):
            ext[0, c, x, 0], ext[0, c, x, 1] = v[c, x], rv[c, x]
            for t in range(3):
                ef[t, c, x, 0], ef[t, c, x, 1] = f[t, c, x], rf[t, c, x]
    own, rim = x_items(comps)

    def put(item, tile, above, value):
        name, c, d = item
        x = jnp.where(above, size_x - 1 + d, wide - d)
        if name == "v":
            ext[0, c, x, tile] = value
        elif name == "nu":
            enu[x, tile] = value
        else:
            ef[name, c, x, tile] = value

    for recv, above in ((recv_a, even), (recv_b, jnp.logical_not(even))):
        for at, item in enumerate(own):
            put(item, 0, above, recv[at])
        for at, (first, second, shift) in enumerate(rim):
            value = recv[len(own) + at]
            put(first, 1, above, value)
            if second is not None:
                put(second, 1, above, unmerge(value, shift))

    def reach(x):
        return 0 if x < size_x else min(x - size_x + 1, wide - x)

    def tiles(limit):
        for x in range(wide):
            for tile in range(2):
                if reach(x) + tile <= limit:
                    yield x, tile

    for x, tile in tiles(DEPTH - 1):
        here, other = enu[x, tile], enu[x, 1 - tile]
        east = 0.5 * (here + enu[(x + 1) % wide, tile])
        west = 0.5 * (here + enu[(x - 1) % wide, tile])
        north = 0.5 * (here + beside_y(here, other, True))
        south = 0.5 * (here + beside_y(here, other, False))
        ahead = jnp.where(lane == 127, 0.0, pltpu.roll(here, 127, 1))
        behind = jnp.where(lane == 0, 0.0, pltpu.roll(here, 1, 1))
        front = 0.5 * (here + ahead)
        back = 0.5 * (here + behind)
        coef[x, tile, 0] = 1.0 - (((east + west) + (north + south)) + (front + back))
        if x == size_x - 1:
            east = east * x_top
        if x == 0:
            west = west * x_low
        if tile == 0:
            north = jnp.where(sub == 7, north * y_top, north)
            south = jnp.where(sub == 0, south * y_low, south)
        coef[x, tile, 1], coef[x, tile, 2] = east, west
        coef[x, tile, 3], coef[x, tile, 4] = north, south
        coef[x, tile, 5] = jnp.where(lane == 127, 0.0, front)
        coef[x, tile, 6] = jnp.where(lane == 0, 0.0, back)

    for t in range(steps):
        src, dst = t % 2, (t + 1) % 2
        for x, tile in tiles(DEPTH - 1 - t):
            w = [coef[x, tile, i] for i in range(7)]
            for c in range(comps):
                here, other = ext[src, c, x, tile], ext[src, c, x, 1 - tile]
                new = w[0] * here
                new = new + w[1] * ext[src, c, (x + 1) % wide, tile]
                new = new + w[2] * ext[src, c, (x - 1) % wide, tile]
                new = new + w[3] * beside_y(here, other, True)
                new = new + w[4] * beside_y(here, other, False)
                new = new + w[5] * pltpu.roll(here, 127, 1)
                new = new + w[6] * pltpu.roll(here, 1, 1)
                push = ef[t, c, x, tile] if t < 3 else f[t, c, x]
                new = new + push
                if t < steps - 1:
                    ext[dst, c, x, tile] = new
                if tile == 0 and x < size_x:
                    snaps[t, c * size_x + x] = new

    last = pltpu.make_async_copy(snaps.at[steps - 1], final, sem.at[0])
    last.start()

    rows = kept.shape[0]
    slabs = kept.shape[1]
    n = rows + steps
    column = lax.broadcasted_iota(jnp.int32, (8, n), 1)
    total = square_a[...] + square_b[...]
    old = 0.5 * total[:, :n] + total[:, n:]
    scale = 1.0 / (slabs * 8 * 128 * nx * ny)
    for k0 in range(0, n, 8):
        acc = [[None] * 8 for _ in range(steps)]
        for s in range(slabs):
            new = [snaps[t, s] for t in range(steps)]
            for k in range(8):
                row = kept[k0 + k, s] if k0 + k < rows else new[k0 + k - rows]
                for t in range(steps):
                    if k0 + k >= rows and k0 + k - rows > t:
                        continue
                    term = row * new[t]
                    acc[t][k] = term if acc[t][k] is None else acc[t][k] + term
        block = old[k0 : k0 + 8]
        for t in range(steps):
            full = jnp.stack([jnp.zeros((8, 128), F32) if a is None else a for a in acc[t]], 0)
            summed = jnp.sum(pltpu.einshape("kyz->ykz", full), axis=0)
            entry = jnp.sum(summed, axis=1, keepdims=True)
            if k0 + 8 > rows:
                row_at = lax.broadcasted_iota(jnp.int32, (8, 1), 0) + k0
                entry = jnp.where(row_at == rows + t, 0.5 * entry, entry)
            block = jnp.where(column == rows + t, entry, block)
        part[pl.ds(k0, 8), :] = block * scale
    last.wait()


def split(p):
    high = p.astype(BF16)
    return high, (p - high.astype(F32)).astype(BF16)


def to_rows(tiles):
    parts = [pltpu.einshape("kyz->ykz", tiles[k : k + 8]) for k in range(0, tiles.shape[0], 8)]
    return [jnp.concatenate([p[y] for p in parts], 0) for y in range(8)]


def from_rows(rows):
    n = rows[0].shape[0]
    return jnp.concatenate(
        [
            pltpu.einshape("ykz->kyz", jnp.stack([r[k : k + 8] for r in rows], 0))
            for k in range(0, n, 8)
        ],
        0,
    )


def square_of(kept, slabs, n, ready=None):
    rows = kept.shape[0]
    acc = None
    for s in slabs:
        if ready is not None:
            ready(s)
        tiles = jnp.concatenate([kept[:, s], jnp.zeros((n - rows, 8, 128), F32)], 0)
        lines = to_rows(tiles)
        for y in range(0, 8, 2):
            high, low = split(jnp.concatenate(lines[y : y + 2], 1))
            both = jnp.concatenate([high, low], 0)
            term = lax.dot_general(high, both, (((1,), (1,)), ((), ())), preferred_element_type=F32)
            acc = term if acc is None else acc + term
    return acc


def square_first_kernel(kept_in, kept, out, sems, *, n, count):
    slabs = kept.shape[1]
    step = slabs // sems.shape[0]
    copies = []
    for i in range(sems.shape[0]):
        at = (slice(None), pl.ds(i * step, step))
        copies.append(pltpu.make_async_copy(kept_in.at[at], kept.at[at], sems.at[i]))
    ahead = 3
    for copy in copies[:ahead]:
        copy.start()

    def arrive(i):
        copies[i].wait()
        if i + ahead < len(copies):
            copies[i + ahead].start()

    def ready(s):
        if s % step == 0:
            arrive(s // step)

    out[...] = square_of(kept, range(count), n, ready)
    for i in range(-(-count // step), len(copies)):
        arrive(i)


def square_rest_kernel(kept, out, *, n, count):
    out[...] = square_of(kept, range(count, kept.shape[1]), n)


def eliminate(w, b):
    sub = sub_index()
    count = len(w)

    def spread(tile, j):
        return jnp.broadcast_to(tile[:, j : j + 1], tile.shape)

    def pick(tile, q):
        return jnp.broadcast_to(tile[q : q + 1, :], tile.shape)

    cols = {c: [spread(w[c], 8 * b + q) for q in range(8)] for c in range(b, count)}
    pivots = jnp.ones(w[b].shape, F32)
    for q in range(8):
        head = [pick(cols[b][r], q) for r in range(q, 8)]
        inverse = 1.0 / head[0]
        pivots = jnp.where(sub == q, head[0], pivots)
        line = pick(w[b], q)
        for c in range(b, count):
            ratio = cols[c][q] * inverse
            if c == b:
                ratio = jnp.where(sub > q, ratio, 0.0)
            w[c] = w[c] - ratio * line
            for r in range(q + 1, 8):
                cols[c][r] = cols[c][r] - ratio * head[r - q]
    w[b] = w[b] * lax.rsqrt(pivots)


def halves_kernel(kept, snaps, panel):
    n = panel.shape[1] // 2
    for s in range(kept.shape[1]):
        lines = to_rows(jnp.concatenate([kept[:, s], snaps[:, s]], 0))
        for i in range(4):
            high, low = split(jnp.concatenate(lines[2 * i : 2 * i + 2], 1))
            panel[4 * s + i, :n], panel[4 * s + i, n:] = high, low


def basis_kernel(part, panel, basis, factor, out, upper, sems, sem):
    n = part.shape[0]
    mid = n // 2
    slabs = panel.shape[0] // 4
    batches = sems.shape[1]
    block = slabs // batches
    m = part[...]
    row_at = lax.broadcasted_iota(jnp.int32, (n, n), 0)
    col_at = lax.broadcasted_iota(jnp.int32, (n, n), 1)
    eye = jnp.where(row_at == col_at, 1.0, 0.0).astype(F32)
    whole = jnp.concatenate([m + m.T, eye], 1)
    w = [whole[c : c + 8] for c in range(0, n, 8)]
    copies = []

    def rows_of(first, last, between):
        inverse = jnp.concatenate(w[first // 8 : last // 8], 0)[:, n : n + last]
        high, low = split(inverse)
        top = jnp.concatenate([high, high], 1)
        lhs = jnp.concatenate([top, jnp.concatenate([low, jnp.zeros_like(low)], 1)], 0)
        for s in range(slabs):
            pieces = []
            for i in range(4):
                high, low = panel[4 * s + i, :last], panel[4 * s + i, n : n + last]
                rhs = jnp.concatenate([high, low], 0)
                r = lax.dot_general(lhs, rhs, (((1,), (0,)), ((), ())), preferred_element_type=F32)
                r = r[: last - first] + r[last - first :]
                pieces += [r[:, :128], r[:, 128:]]
            out[first:last, s] = from_rows(pieces)
            between(s)
            if (s + 1) % block == 0:
                at = (pl.ds(first, last - first), pl.ds(s + 1 - block, block))
                sem = sems.at[0 if first == 0 else 1, s // block]
                copy = pltpu.make_async_copy(out.at[at], basis.at[at], sem)
                copy.start()
                copies.append(copy)

    half = mid // 8
    for b in range(half):
        eliminate(w, b)
    pace = slabs // half

    def go_on(s):
        if (s + 1) % pace == 0 and (s + 1) // pace <= half:
            eliminate(w, half + (s + 1) // pace - 1)

    rows_of(0, mid, go_on)
    upper[...] = jnp.where(row_at <= col_at, jnp.concatenate(w, 0)[:, :n], 0.0)
    copies.append(pltpu.make_async_copy(upper, factor, sem.at[0]))
    copies[-1].start()
    rows_of(mid, n, lambda s: None)
    for copy in copies:
        copy.wait()


def pair_exchange(first, second, axis):
    count = lax.axis_size(axis)
    near = [(i, i ^ 1) for i in range(count)]
    far = [(i, ((i + 1) ^ 1) - 1) for i in range(1, count - 1)]
    distant = lax.ppermute(second, axis, far)
    return lax.ppermute(first, axis, near), distant


def sum_over(value, minor, major):
    inner, outer = lax.axis_size(minor), lax.axis_size(major)
    count = inner * outer
    if count & (count - 1):
        return lax.psum(value, (major, minor))
    low = [1 << i for i in range(inner.bit_length() - 1)]
    high = [inner << i for i in range(outer.bit_length() - 1)]
    both = min(len(low), len(high))
    groups = [[high[i], low[i]] for i in range(both)]
    rest = low[both:] + high[both:]
    groups += [rest[i : i + 2] for i in range(0, len(rest), 2)]
    for group in groups:
        masks = group + ([group[0] ^ group[1]] if len(group) == 2 else [])
        others = [
            lax.ppermute(value, (major, minor), [(i, i ^ m) for i in range(count)]) for m in masks
        ]
        for other in others:
            value = value + other
    return value


def local(velocity, viscosity, forcing, earlier):
    comps, size_x = velocity.shape[0], velocity.shape[1]
    steps, rows = forcing.shape[0], earlier.shape[0]
    n, slabs = rows + steps, comps * size_x
    half = (2 * slabs + size_x + slabs // 2) // 2
    call = pl.pallas_call
    v, nu, f, send_a, send_b = call(
        pack_y_kernel,
        out_shape=(
            struct(*velocity.shape),
            struct(*viscosity.shape),
            struct(*forcing.shape),
            struct(half, 8, 128),
            struct(half, 8, 128),
        ),
        in_specs=[HBM] * 3,
        out_specs=(VMEM,) * 5,
        scratch_shapes=[pltpu.SemaphoreType.DMA((3,))],
        compiler_params=limit(8),
        name="pack_y",
    )(*[pltpu.with_memory_space_constraint(a, pltpu.HBM) for a in (velocity, viscosity, forcing)])
    recv_a, recv_b = pair_exchange(send_a, send_b, "gy")
    first = slabs * 2 // 3
    kept, square_a = call(
        functools.partial(square_first_kernel, n=n, count=first),
        out_shape=(struct(rows, slabs, 8, 128), struct(n, 2 * n)),
        in_specs=[HBM],
        out_specs=(VMEM,) * 2,
        scratch_shapes=[pltpu.SemaphoreType.DMA((6,))],
        compiler_params=limit(8),
        name="gram_first",
    )(pltpu.with_memory_space_constraint(earlier.reshape(rows, slabs, 8, 128), pltpu.HBM))
    own, rim = x_items(comps)
    wire = struct(len(own) + len(rim), 8, 128)
    rv, rnu, rf, send_a, send_b = call(
        pack_x_kernel,
        out_shape=(
            struct(*velocity.shape),
            struct(*viscosity.shape),
            struct(3, *velocity.shape),
            wire,
            wire,
        ),
        in_specs=[VMEM] * 5 + [pl.BlockSpec(memory_space=pl.ANY)],
        out_specs=(VMEM,) * 5,
        compiler_params=limit(8),
        name="pack_x",
    )(v, nu, f, recv_a, recv_b, square_a)
    recv_a, recv_b = pair_exchange(send_a, send_b, "gx")
    square_b = call(
        functools.partial(square_rest_kernel, n=n, count=first),
        out_shape=struct(n, 2 * n),
        in_specs=[VMEM],
        out_specs=VMEM,
        compiler_params=limit(8),
        name="gram_rest",
    )(kept)
    snaps, final, part = call(
        steps_kernel,
        out_shape=(struct(steps, slabs, 8, 128), struct(slabs, 8, 128), struct(n, n)),
        in_specs=[VMEM] * 11,
        out_specs=(VMEM, HBM, VMEM),
        scratch_shapes=[
            pltpu.VMEM((2, comps, 2 * size_x, 2, 8, 128), F32),
            pltpu.VMEM((2 * size_x, 2, 8, 128), F32),
            pltpu.VMEM((3, comps, 2 * size_x, 2, 8, 128), F32),
            pltpu.VMEM((2 * size_x, 2, 7, 8, 128), F32),
            pltpu.SemaphoreType.DMA((1,)),
        ],
        compiler_params=limit(12),
        name="steps",
    )(v, nu, f, rv, rnu, rf, recv_a, recv_b, kept, square_a, square_b)
    panel = call(
        halves_kernel,
        out_shape=jax.ShapeDtypeStruct((4 * slabs, 2 * n, 256), BF16),
        in_specs=[VMEM] * 2,
        out_specs=VMEM,
        compiler_params=limit(8),
        name="halves",
    )(kept, snaps)
    part = sum_over(part, "gy", "gx")
    basis, factor = call(
        basis_kernel,
        out_shape=(struct(n, slabs, 8, 128), struct(n, n)),
        in_specs=[VMEM] * 2,
        out_specs=(HBM, HBM),
        scratch_shapes=[
            pltpu.VMEM((n, slabs, 8, 128), F32),
            pltpu.VMEM((n, n), F32),
            pltpu.SemaphoreType.DMA((2, slabs // 3)),
            pltpu.SemaphoreType.DMA((1,)),
        ],
        compiler_params=limit(16),
        name="factor_basis",
    )(part, panel)
    return final.reshape(velocity.shape), basis.reshape((n,) + velocity.shape), factor


def solution(mesh):
    return jax.shard_map(
        local,
        mesh=mesh,
        in_specs=(
            P(None, "gx", "gy", None),
            P("gx", "gy", None),
            P(None, None, "gx", "gy", None),
            P(None, None, "gx", "gy", None),
        ),
        out_specs=(P(None, "gx", "gy", None), P(None, None, "gx", "gy", None), P()),
        check_vma=False,
    )
```

```python
import functools
import jax
import jax.numpy as jnp
from jax import lax
from jax.experimental import pallas as pl
from jax.experimental.pallas import tpu as pltpu
from jax.sharding import PartitionSpec as P

F32 = jnp.float32
BF16 = jnp.bfloat16
DEPTH = 4
VMEM = pl.BlockSpec(memory_space=pltpu.VMEM)
HBM = pl.BlockSpec(memory_space=pltpu.HBM)


def limit(mib):
    return pltpu.CompilerParams(vmem_limit_bytes=mib << 20)


def struct(*shape):
    return jax.ShapeDtypeStruct(shape, F32)


def sub_index():
    return lax.broadcasted_iota(jnp.int32, (8, 128), 0)


def turn(tile, shift):
    return pltpu.roll(tile, shift, 0)


def y_items(v, nu, f, up):
    sub = sub_index()
    comps, size_x = v.shape[0], v.shape[1]
    cells = [(c, x) for c in range(comps) for x in range(size_x)]
    items = [v[c, x] for c, x in cells] + [nu[x] for x in range(size_x)]
    for c, x in cells:
        if up:
            items.append(jnp.where(sub == 4, turn(f[2, c, x], 5), f[0, c, x]))
        else:
            items.append(jnp.where(sub == 3, turn(f[2, c, x], 3), f[0, c, x]))
    for (c, x), (d, w) in zip(cells[0::2], cells[1::2]):
        if up:
            items.append(jnp.where(sub >= 6, f[1, c, x], turn(f[1, d, w], 6)))
        else:
            items.append(jnp.where(sub < 2, f[1, c, x], turn(f[1, d, w], 2)))
    return items


def pack_y_kernel(v_in, nu_in, f_in, v, nu, f, send_a, send_b, sems):
    pairs = ((f_in, f), (v_in, v), (nu_in, nu))
    copies = [pltpu.make_async_copy(a, b, sems.at[i]) for i, (a, b) in enumerate(pairs)]
    for copy in copies:
        copy.start()
    for copy in copies:
        copy.wait()
    sub = sub_index()
    even = lax.rem(lax.axis_index("gy"), 2) == 0
    upper, lower = (y_items(v, nu, f, True), y_items(v, nu, f, False))
    half = send_a.shape[0]
    for j in range(half):
        to_up = jnp.where(sub >= 4, upper[j], turn(upper[half + j], 4))
        to_down = jnp.where(sub < 4, lower[j], turn(lower[half + j], 4))
        send_a[j] = jnp.where(even, to_up, to_down)
        send_b[j] = jnp.where(even, to_down, to_up)


def unpack_y(recv_a, recv_b, even, j):
    sub = sub_index()
    half = recv_a.shape[0]
    k = j % half
    a, b = recv_a[k], recv_b[k]
    above, below = jnp.where(even, a, b), jnp.where(even, b, a)
    if j < half:
        return jnp.where(sub < 4, above, below)
    return turn(jnp.where(sub < 4, below, above), 4)


def x_items(comps):
    own = [("v", c, d) for c in range(comps) for d in range(1, 5)]
    own += [("nu", 0, d) for d in range(1, 5)]
    for t in range(3):
        own += [(t, c, d) for c in range(comps) for d in range(1, 4 - t)]
    fields = [("v", c) for c in range(comps)] + [("nu", 0)]
    rim = [((name, c, 1), (name, c, 3), 3) for name, c in fields]
    four = [(name, c, 2) for name, c in fields] + [(0, c, 1) for c in range(comps)]
    four += [(0, c, 2) for c in range(comps)] + [(1, c, 1) for c in range(comps)]
    rim += [(one, two, 2) for one, two in zip(four[0::2], four[1::2])]
    rim += [(one, None, 0) for one in four[len(four) - len(four) % 2 :]]
    return own, rim


def merge(first, second, shift):
    sub = sub_index()
    if shift == 3:
        above, below = sub == 3, sub == 4
    else:
        above, below = (sub >= 2) & (sub < 4), (sub >= 4) & (sub < 6)
    return jnp.where(above, turn(second, shift), jnp.where(below, turn(second, 8 - shift), first))


def unmerge(tile, shift):
    return jnp.where(sub_index() < 4, turn(tile, 8 - shift), turn(tile, shift))


def pack_x_kernel(v, nu, f, recv_a, recv_b, after, rv, rnu, rf, send_a, send_b):
    sub = sub_index()
    even_y = lax.rem(lax.axis_index("gy"), 2) == 0
    even_x = lax.rem(lax.axis_index("gx"), 2) == 0
    comps, size_x = v.shape[0], v.shape[1]
    cells = [(c, x) for c in range(comps) for x in range(size_x)]
    get = functools.partial(unpack_y, recv_a, recv_b, even_y)
    at = 0
    for c, x in cells:
        rv[c, x] = get(at)
        at += 1
    for x in range(size_x):
        rnu[x] = get(at)
        at += 1
    for c, x in cells:
        item = get(at)
        rf[0, c, x] = item
        rf[2, c, x] = jnp.where(sub < 4, turn(item, 5), turn(item, 3))
        at += 1
    for (c, x), (d, w) in zip(cells[0::2], cells[1::2]):
        item = get(at)
        rf[1, c, x] = item
        rf[1, d, w] = jnp.where(sub < 4, turn(item, 6), turn(item, 2))
        at += 1
    own, rim = x_items(comps)

    def take(source, item, upward):
        name, c, d = item
        field, viscosity, push = source
        x = jnp.where(upward, size_x - d, d - 1)
        if name == "v":
            return field[c, x]
        return viscosity[x] if name == "nu" else push[name, c, x]

    for send, upward in ((send_a, even_x), (send_b, jnp.logical_not(even_x))):
        for at, item in enumerate(own):
            send[at] = take((v, nu, f), item, upward)
        for at, (one, two, shift) in enumerate(rim):
            tile = take((rv, rnu, rf), one, upward)
            if two is not None:
                tile = merge(tile, take((rv, rnu, rf), two, upward), shift)
            send[len(own) + at] = tile


def beside_y(first, second, up):
    sub = sub_index()
    if up:
        return jnp.where(sub == 7, turn(second, 7), turn(first, 7))
    return jnp.where(sub == 0, turn(second, 1), turn(first, 1))


def steps_kernel(v, nu, f, rv, rnu, rf, recv_a, recv_b, kept, square_a, square_b, snaps, final, part, ext, enu, ef, coef, sem):
    comps, size_x = v.shape[0], v.shape[1]
    steps = f.shape[0]
    wide = 2 * size_x
    ix, nx = lax.axis_index("gx"), lax.axis_size("gx")
    iy, ny = lax.axis_index("gy"), lax.axis_size("gy")
    even = lax.rem(ix, 2) == 0
    sub = sub_index()
    lane = lax.broadcasted_iota(jnp.int32, (8, 128), 1)
    one = lambda flag: jnp.where(flag, 1.0, 0.0).astype(F32)
    x_top, x_low = one(ix < nx - 1), one(ix > 0)
    y_top, y_low = one(iy < ny - 1), one(iy > 0)

    for x in range(size_x):
        enu[x, 0], enu[x, 1] = nu[x], rnu[x]
        for c in range(comps):
            ext[0, c, x, 0], ext[0, c, x, 1] = v[c, x], rv[c, x]
            for t in range(3):
                ef[t, c, x, 0], ef[t, c, x, 1] = f[t, c, x], rf[t, c, x]
    own, rim = x_items(comps)

    def put(item, tile, above, value):
        name, c, d = item
        x = jnp.where(above, size_x - 1 + d, wide - d)
        if name == "v":
            ext[0, c, x, tile] = value
        elif name == "nu":
            enu[x, tile] = value
        else:
            ef[name, c, x, tile] = value

    for recv, above in ((recv_a, even), (recv_b, jnp.logical_not(even))):
        for at, item in enumerate(own):
            put(item, 0, above, recv[at])
        for at, (first, second, shift) in enumerate(rim):
            value = recv[len(own) + at]
            put(first, 1, above, value)
            if second is not None:
                put(second, 1, above, unmerge(value, shift))

    def reach(x):
        return 0 if x < size_x else min(x - size_x + 1, wide - x)

    def tiles(limit):
        for x in range(wide):
            for tile in range(2):
                if reach(x) + tile <= limit:
                    yield x, tile

    for x, tile in tiles(DEPTH - 1):
        here, other = enu[x, tile], enu[x, 1 - tile]
        east = 0.5 * (here + enu[(x + 1) % wide, tile])
        west = 0.5 * (here + enu[(x - 1) % wide, tile])
        north = 0.5 * (here + beside_y(here, other, True))
        south = 0.5 * (here + beside_y(here, other, False))
        ahead = jnp.where(lane == 127, 0.0, pltpu.roll(here, 127, 1))
        behind = jnp.where(lane == 0, 0.0, pltpu.roll(here, 1, 1))
        front = 0.5 * (here + ahead)
        back = 0.5 * (here + behind)
        coef[x, tile, 0] = 1.0 - (((east + west) + (north + south)) + (front + back))
        if x == size_x - 1:
            east = east * x_top
        if x == 0:
            west = west * x_low
        if tile == 0:
            north = jnp.where(sub == 7, north * y_top, north)
            south = jnp.where(sub == 0, south * y_low, south)
        coef[x, tile, 1], coef[x, tile, 2] = east, west
        coef[x, tile, 3], coef[x, tile, 4] = north, south
        coef[x, tile, 5] = jnp.where(lane == 127, 0.0, front)
        coef[x, tile, 6] = jnp.where(lane == 0, 0.0, back)

    for t in range(steps):
        src, dst = t % 2, (t + 1) % 2
        for x, tile in tiles(DEPTH - 1 - t):
            w = [coef[x, tile, i] for i in range(7)]
            for c in range(comps):
                here, other = ext[src, c, x, tile], ext[src, c, x, 1 - tile]
                new = w[0] * here
                new = new + w[1] * ext[src, c, (x + 1) % wide, tile]
                new = new + w[2] * ext[src, c, (x - 1) % wide, tile]
                new = new + w[3] * beside_y(here, other, True)
                new = new + w[4] * beside_y(here, other, False)
                new = new + w[5] * pltpu.roll(here, 127, 1)
                new = new + w[6] * pltpu.roll(here, 1, 1)
                push = ef[t, c, x, tile] if t < 3 else f[t, c, x]
                new = new + push
                if t < steps - 1:
                    ext[dst, c, x, tile] = new
                if tile == 0 and x < size_x:
                    snaps[t, c * size_x + x] = new

    last = pltpu.make_async_copy(snaps.at[steps - 1], final, sem.at[0])
    last.start()

    rows = kept.shape[0]
    slabs = kept.shape[1]
    n = rows + steps
    column = lax.broadcasted_iota(jnp.int32, (8, n), 1)
    total = square_a[...] + square_b[...]
    old = 0.5 * total[:, :n] + total[:, n:]
    scale = 1.0 / (slabs * 8 * 128 * nx * ny)
    for k0 in range(0, n, 8):
        acc = [[None] * 8 for _ in range(steps)]
        for s in range(slabs):
            new = [snaps[t, s] for t in range(steps)]
            for k in range(8):
                row = kept[k0 + k, s] if k0 + k < rows else new[k0 + k - rows]
                for t in range(steps):
                    if k0 + k >= rows and k0 + k - rows > t:
                        continue
                    term = row * new[t]
                    acc[t][k] = term if acc[t][k] is None else acc[t][k] + term
        block = old[k0 : k0 + 8]
        for t in range(steps):
            full = jnp.stack([jnp.zeros((8, 128), F32) if a is None else a for a in acc[t]], 0)
            summed = jnp.sum(pltpu.einshape("kyz->ykz", full), axis=0)
            entry = jnp.sum(summed, axis=1, keepdims=True)
            if k0 + 8 > rows:
                row_at = lax.broadcasted_iota(jnp.int32, (8, 1), 0) + k0
                entry = jnp.where(row_at == rows + t, 0.5 * entry, entry)
            block = jnp.where(column == rows + t, entry, block)
        part[pl.ds(k0, 8), :] = block * scale
    last.wait()


def split(p):
    high = p.astype(BF16)
    return high, (p - high.astype(F32)).astype(BF16)


def to_rows(tiles):
    parts = [pltpu.einshape("kyz->ykz", tiles[k : k + 8]) for k in range(0, tiles.shape[0], 8)]
    return [jnp.concatenate([p[y] for p in parts], 0) for y in range(8)]


def from_rows(rows):
    n = rows[0].shape[0]
    return jnp.concatenate(
        [
            pltpu.einshape("ykz->kyz", jnp.stack([r[k : k + 8] for r in rows], 0))
            for k in range(0, n, 8)
        ],
        0,
    )


def square_of(kept, slabs, n, ready=None):
    rows = kept.shape[0]
    acc = None
    for s in slabs:
        if ready is not None:
            ready(s)
        tiles = jnp.concatenate([kept[:, s], jnp.zeros((n - rows, 8, 128), F32)], 0)
        lines = to_rows(tiles)
        for y in range(0, 8, 2):
            high, low = split(jnp.concatenate(lines[y : y + 2], 1))
            both = jnp.concatenate([high, low], 0)
            term = lax.dot_general(high, both, (((1,), (1,)), ((), ())), preferred_element_type=F32)
            acc = term if acc is None else acc + term
    return acc


def square_first_kernel(kept_in, kept, out, sems, *, n, count):
    slabs = kept.shape[1]
    step = slabs // sems.shape[0]
    copies = []
    for i in range(sems.shape[0]):
        at = (slice(None), pl.ds(i * step, step))
        copies.append(pltpu.make_async_copy(kept_in.at[at], kept.at[at], sems.at[i]))
    ahead = 3
    for copy in copies[:ahead]:
        copy.start()

    def arrive(i):
        copies[i].wait()
        if i + ahead < len(copies):
            copies[i + ahead].start()

    def ready(s):
        if s % step == 0:
            arrive(s // step)

    out[...] = square_of(kept, range(count), n, ready)
    for i in range(-(-count // step), len(copies)):
        arrive(i)


def square_rest_kernel(kept, out, *, n, count):
    out[...] = square_of(kept, range(count, kept.shape[1]), n)


def eliminate(w, b):
    sub = sub_index()
    count = len(w)

    def spread(tile, j):
        return jnp.broadcast_to(tile[:, j : j + 1], tile.shape)

    def pick(tile, q):
        return jnp.broadcast_to(tile[q : q + 1, :], tile.shape)

    cols = {c: [spread(w[c], 8 * b + q) for q in range(8)] for c in range(b, count)}
    pivots = jnp.ones(w[b].shape, F32)
    for q in range(8):
        head = [pick(cols[b][r], q) for r in range(q, 8)]
        inverse = 1.0 / head[0]
        pivots = jnp.where(sub == q, head[0], pivots)
        line = pick(w[b], q)
        for c in range(b, count):
            ratio = cols[c][q] * inverse
            if c == b:
                ratio = jnp.where(sub > q, ratio, 0.0)
            w[c] = w[c] - ratio * line
            for r in range(q + 1, 8):
                cols[c][r] = cols[c][r] - ratio * head[r - q]
    w[b] = w[b] * lax.rsqrt(pivots)


def halves_kernel(kept, snaps, panel):
    n = panel.shape[1] // 2
    for s in range(kept.shape[1]):
        lines = to_rows(jnp.concatenate([kept[:, s], snaps[:, s]], 0))
        for i in range(4):
            high, low = split(jnp.concatenate(lines[2 * i : 2 * i + 2], 1))
            panel[4 * s + i, :n], panel[4 * s + i, n:] = high, low


def basis_kernel(part, panel, basis, factor, out, upper, sems, sem):
    n = part.shape[0]
    mid = n // 2
    slabs = panel.shape[0] // 4
    batches = sems.shape[1]
    block = slabs // batches
    m = part[...]
    row_at = lax.broadcasted_iota(jnp.int32, (n, n), 0)
    col_at = lax.broadcasted_iota(jnp.int32, (n, n), 1)
    eye = jnp.where(row_at == col_at, 1.0, 0.0).astype(F32)
    whole = jnp.concatenate([m + m.T, eye], 1)
    w = [whole[c : c + 8] for c in range(0, n, 8)]
    copies = []

    def rows_of(first, last, between):
        inverse = jnp.concatenate(w[first // 8 : last // 8], 0)[:, n : n + last]
        high, low = split(inverse)
        top = jnp.concatenate([high, high], 1)
        lhs = jnp.concatenate([top, jnp.concatenate([low, jnp.zeros_like(low)], 1)], 0)
        for s in range(slabs):
            pieces = []
            for i in range(4):
                high, low = panel[4 * s + i, :last], panel[4 * s + i, n : n + last]
                rhs = jnp.concatenate([high, low], 0)
                r = lax.dot_general(lhs, rhs, (((1,), (0,)), ((), ())), preferred_element_type=F32)
                r = r[: last - first] + r[last - first :]
                pieces += [r[:, :128], r[:, 128:]]
            out[first:last, s] = from_rows(pieces)
            between(s)
            if (s + 1) % block == 0:
                at = (pl.ds(first, last - first), pl.ds(s + 1 - block, block))
                sem = sems.at[0 if first == 0 else 1, s // block]
                copy = pltpu.make_async_copy(out.at[at], basis.at[at], sem)
                copy.start()
                copies.append(copy)

    half = mid // 8
    for b in range(half):
        eliminate(w, b)
    pace = slabs // half

    def go_on(s):
        if (s + 1) % pace == 0 and (s + 1) // pace <= half:
            eliminate(w, half + (s + 1) // pace - 1)

    rows_of(0, mid, go_on)
    upper[...] = jnp.where(row_at <= col_at, jnp.concatenate(w, 0)[:, :n], 0.0)
    copies.append(pltpu.make_async_copy(upper, factor, sem.at[0]))
    copies[-1].start()
    rows_of(mid, n, lambda s: None)
    for copy in copies:
        copy.wait()


def pair_exchange(first, second, axis):
    count = lax.axis_size(axis)
    near = [(i, i ^ 1) for i in range(count)]
    far = [(i, ((i + 1) ^ 1) - 1) for i in range(1, count - 1)]
    distant = lax.ppermute(second, axis, far)
    return lax.ppermute(first, axis, near), distant


def sum_over(value, minor, major, beside):
    inner, outer = lax.axis_size(minor), lax.axis_size(major)
    count = inner * outer
    if count & (count - 1):
        return lax.psum(value, (major, minor)), beside
    low = [1 << i for i in range(inner.bit_length() - 1)]
    high = [inner << i for i in range(outer.bit_length() - 1)]
    both = min(len(low), len(high))
    groups = [[high[i], low[i]] for i in range(both)]
    rest = low[both:] + high[both:]
    groups += [rest[i : i + 2] for i in range(0, len(rest), 2)]
    for at, group in enumerate(groups):
        if at == len(groups) - 1:
            value, beside = lax.optimization_barrier((value, beside))
        masks = group + ([group[0] ^ group[1]] if len(group) == 2 else [])
        others = [
            lax.ppermute(value, (major, minor), [(i, i ^ m) for i in range(count)]) for m in masks
        ]
        for other in others:
            value = value + other
    return value, beside


def local(velocity, viscosity, forcing, earlier):
    comps, size_x = velocity.shape[0], velocity.shape[1]
    steps, rows = forcing.shape[0], earlier.shape[0]
    n, slabs = rows + steps, comps * size_x
    half = (2 * slabs + size_x + slabs // 2) // 2
    call = pl.pallas_call
    v, nu, f, send_a, send_b = call(
        pack_y_kernel,
        out_shape=(
            struct(*velocity.shape),
            struct(*viscosity.shape),
            struct(*forcing.shape),
            struct(half, 8, 128),
            struct(half, 8, 128),
        ),
        in_specs=[HBM] * 3,
        out_specs=(VMEM,) * 5,
        scratch_shapes=[pltpu.SemaphoreType.DMA((3,))],
        compiler_params=limit(8),
        name="pack_y",
    )(*[pltpu.with_memory_space_constraint(a, pltpu.HBM) for a in (velocity, viscosity, forcing)])
    recv_a, recv_b = pair_exchange(send_a, send_b, "gy")
    first = slabs * 2 // 3
    kept, square_a = call(
        functools.partial(square_first_kernel, n=n, count=first),
        out_shape=(struct(rows, slabs, 8, 128), struct(n, 2 * n)),
        in_specs=[HBM],
        out_specs=(VMEM,) * 2,
        scratch_shapes=[pltpu.SemaphoreType.DMA((6,))],
        compiler_params=limit(8),
        name="gram_first",
    )(pltpu.with_memory_space_constraint(earlier.reshape(rows, slabs, 8, 128), pltpu.HBM))
    own, rim = x_items(comps)
    wire = struct(len(own) + len(rim), 8, 128)
    rv, rnu, rf, send_a, send_b = call(
        pack_x_kernel,
        out_shape=(
            struct(*velocity.shape),
            struct(*viscosity.shape),
            struct(3, *velocity.shape),
            wire,
            wire,
        ),
        in_specs=[VMEM] * 5 + [pl.BlockSpec(memory_space=pl.ANY)],
        out_specs=(VMEM,) * 5,
        compiler_params=limit(8),
        name="pack_x",
    )(v, nu, f, recv_a, recv_b, square_a)
    recv_a, recv_b = pair_exchange(send_a, send_b, "gx")
    square_b = call(
        functools.partial(square_rest_kernel, n=n, count=first),
        out_shape=struct(n, 2 * n),
        in_specs=[VMEM],
        out_specs=VMEM,
        compiler_params=limit(8),
        name="gram_rest",
    )(kept)
    snaps, final, part = call(
        steps_kernel,
        out_shape=(struct(steps, slabs, 8, 128), struct(slabs, 8, 128), struct(n, n)),
        in_specs=[VMEM] * 11,
        out_specs=(VMEM, HBM, VMEM),
        scratch_shapes=[
            pltpu.VMEM((2, comps, 2 * size_x, 2, 8, 128), F32),
            pltpu.VMEM((2 * size_x, 2, 8, 128), F32),
            pltpu.VMEM((3, comps, 2 * size_x, 2, 8, 128), F32),
            pltpu.VMEM((2 * size_x, 2, 7, 8, 128), F32),
            pltpu.SemaphoreType.DMA((1,)),
        ],
        compiler_params=limit(12),
        name="steps",
    )(v, nu, f, rv, rnu, rf, recv_a, recv_b, kept, square_a, square_b)
    panel = call(
        halves_kernel,
        out_shape=jax.ShapeDtypeStruct((4 * slabs, 2 * n, 256), BF16),
        in_specs=[VMEM] * 2,
        out_specs=VMEM,
        compiler_params=limit(8),
        name="halves",
    )(kept, snaps)
    part, panel = sum_over(part, "gy", "gx", panel)
    basis, factor = call(
        basis_kernel,
        out_shape=(struct(n, slabs, 8, 128), struct(n, n)),
        in_specs=[VMEM] * 2,
        out_specs=(HBM, HBM),
        scratch_shapes=[
            pltpu.VMEM((n, slabs, 8, 128), F32),
            pltpu.VMEM((n, n), F32),
            pltpu.SemaphoreType.DMA((2, slabs // 3)),
            pltpu.SemaphoreType.DMA((1,)),
        ],
        compiler_params=limit(16),
        name="factor_basis",
    )(part, panel)
    return final.reshape(velocity.shape), basis.reshape((n,) + velocity.shape), factor


def solution(mesh):
    return jax.shard_map(
        local,
        mesh=mesh,
        in_specs=(
            P(None, "gx", "gy", None),
            P("gx", "gy", None),
            P(None, None, "gx", "gy", None),
            P(None, None, "gx", "gy", None),
        ),
        out_specs=(P(None, "gx", "gy", None), P(None, None, "gx", "gy", None), P()),
        check_vma=False,
    )
```
